128 devices in a mesh: rep: 2 (over core), tensor: 64 (over x, z, y).
Axes of the slice: x: 4, y: 4, z: 4, core: 2. Of those that a mesh axis runs over, the one named last changes fastest.
Arguments:
- amplitudes: bfloat16 [4, 1600, 3200], P('rep', 'tensor'), may hold values from -6 to 6
- intermediate: bfloat16 [128, 200, 6400], P('tensor', None, 'rep'), may hold values from -0.21875 to 0.21875
- occ_irrep: int32 [200], replicated, may hold values from 0 to 7
- i_window: int32 [16], replicated, may hold values from 0 to 199
- j_window: int32 [128], replicated, may hold values from 0 to 199
- k_window: int32 [4], replicated, may hold values from 0 to 199
- occ_energy: float32 [200], replicated, may hold values from -1 to -0.3
- virt_energy: float32 [1600], replicated, may hold values from 0.2 to 3
Outputs:
- update: bfloat16 [16, 1600, 25600], P('rep', 'tensor')
The draws below stay inside these ranges and needn't reach their ends.
Inputs may be any that keep to these rules, and one draw needn't show every extreme that they name: `i_window`: occupied orbital numbers, repeats possible. `j_window`: occupied orbital numbers, repeats possible. `k_window`: occupied orbital numbers, repeats possible.
All inputs are finite; a program needn't handle non-finite values.
Results may differ from the reference program's by a relative error of at most 0.0058.
Values may be sent and summed in bfloat16 or wider, within the bound.
A program may use at most 320 MiB of HBM per device.

```python
import math
import jax
import jax.numpy as jnp
from jax import lax

IRREPS = 8
V = 1600
O = 200
IB = 16
KG = 2
VH = 200
KB = 4
JB = 128
REPLICAS = 2


def place_ends(drawn, rng, least, high):
    dims = drawn.shape
    place = [jax.random.randint(jax.random.fold_in(rng, axis), (), 0, dims[axis]) for axis in range(len(dims))]
    drawn = drawn.at[tuple(place)].set(least)
    longest = dims.index(max(dims))
    place[longest] = (place[longest] + 1) % dims[longest]
    return drawn.at[tuple(place)].set(high)


def block_levels(stream_key, dims, pieces, low, largest):
    loudness, own = 1.0, jax.random.fold_in(stream_key, 6)
    for dim, shards_of in pieces:
        steps = jnp.exp(jax.random.uniform(jax.random.fold_in(own, dim), (shards_of,), jnp.float32, low / len(pieces), largest / len(pieces)))
        loudness = loudness * jnp.repeat(steps, dims[dim] // shards_of).reshape([-1 if axis == dim else 1 for axis in range(len(dims))])
    return loudness


def centred(own_key, dims, scale, limit, pieces=(), held_as=jnp.bfloat16):
    values = jax.random.normal(own_key, dims, jnp.float32) * scale
    if len(pieces) > 0:
        values = block_levels(own_key, dims, pieces, -0.22, 0.18) * values
    return jnp.clip(values, min=-limit, max=limit).astype(held_as)


def setup_inputs(seed: int = 0) -> dict:
    splits = jax.random.split(jax.random.key(seed), 9)
    amplitudes = centred(splits[0], (KB, V, IB * VH), 1.0, 6.0, ((0, 2), (1, 64)))
    intermediate = centred(splits[1], (JB, VH, KB * V), (KB * VH) ** -0.5, 0.21875, ((0, 64), (2, 2)))
    occ_irrep = place_ends(jax.random.randint(splits[2], (O,), 0, IRREPS), jax.random.fold_in(splits[2], 1), 0, IRREPS - 1).astype(jnp.int32)
    i_window = place_ends(jax.random.randint(splits[3], (IB,), 0, O), jax.random.fold_in(splits[3], 1), 0, O - 1).astype(jnp.int32)
    j_window = place_ends(jax.random.randint(splits[4], (JB,), 0, O), jax.random.fold_in(splits[4], 1), 0, O - 1).astype(jnp.int32)
    k_window = place_ends(jax.random.randint(splits[5], (KB,), 0, O), jax.random.fold_in(splits[5], 1), 0, O - 1).astype(jnp.int32)
    occ_energy = jnp.clip(jax.random.uniform(splits[6], (O,), jnp.float32, -1.0, -0.3), -1.0, -0.3)
    virt_energy = jnp.clip(jnp.exp(jax.random.uniform(splits[7], (V,), jnp.float32, math.log(0.2), math.log(3.0))), 0.2, 3.0)
    return {"amplitudes": amplitudes, "intermediate": intermediate, "occ_irrep": occ_irrep, "i_window": i_window, "j_window": j_window, "k_window": k_window, "occ_energy": occ_energy, "virt_energy": virt_energy}


def reference(amplitudes, intermediate, occ_irrep, i_window, j_window, k_window, occ_energy, virt_energy):
    sym_i = occ_irrep[i_window]
    sym_j = occ_irrep[j_window]
    sym_k = occ_irrep[k_window]
    amp_rows = amplitudes.reshape(KB, V, IB, VH).transpose(2, 0, 1, 3)
    blocks_w = intermediate.reshape(JB * VH, KB, IRREPS, VH)
    energy_table = virt_energy.reshape(IRREPS, VH)
    virt_irrep = jnp.arange(V, dtype=jnp.int32) // VH
    energy_j = occ_energy[j_window]
    irrep_range = jnp.arange(IRREPS, dtype=jnp.int32)

    def per_row(inputs):
        amp_row, sym_row, energy_row = inputs
        summed = jnp.zeros((V, JB * VH), jnp.float32)
        for group_index in range(REPLICAS):
            def add_one(accum, k_local):
                k_index = group_index * KG + k_local
                permute = jnp.bitwise_xor(irrep_range, jnp.bitwise_xor(sym_row, sym_k[k_index]))
                w_block = lax.dynamic_index_in_dim(blocks_w, k_index, 1, keepdims=False)[:, permute]
                a_block = lax.dynamic_index_in_dim(amp_row, k_index, 0, keepdims=False).reshape(IRREPS, VH, VH)
                product = jnp.einsum('hac,nhc->han', a_block.astype(jnp.float32), w_block.astype(jnp.float32))
                return accum + product.reshape(V, JB * VH), None
            partial_sum, _ = lax.scan(add_one, jnp.zeros((V, JB * VH), jnp.float32), jnp.arange(KG, dtype=jnp.int32))
            summed = summed + lax.optimization_barrier(partial_sum.astype(jnp.bfloat16)).astype(jnp.float32)
        contracted = lax.optimization_barrier(summed.astype(jnp.bfloat16))
        contracted = contracted.reshape(V, JB, VH)
        irrep_b = jnp.bitwise_xor(virt_irrep[:, None], jnp.bitwise_xor(sym_row, sym_j)[None, :])
        energy_b = energy_table[irrep_b]
        denominator = energy_row + energy_j[None, :, None] - virt_energy[:, None, None] - energy_b
        result = (contracted.astype(jnp.float32) / denominator).astype(jnp.bfloat16)
        return result.reshape(V, JB * VH)

    return lax.map(per_row, (amp_rows, sym_i, occ_energy[i_window]))
```

```python
import functools
import jax
import jax.numpy as jnp
from jax import lax
from jax.experimental import pallas as pl
from jax.experimental.pallas import tpu as pltpu
from jax.sharding import PartitionSpec as P

IRREPS = 8
VH = 200
ROWS = 25
HALF = 8
PLANE = 16
RING = 4
COLS = 400
LANES = 128
MAIN = 384
TILES = 13
WIN = TILES * LANES
PIECES = 79
PAD = 64
BLOCK = 64
MESH = pl.DeviceIdType.MESH
F32 = jnp.float32
BF16 = jnp.bfloat16
ORDER = (
    (0, 1, 2, 3, 4, 5, 10, 11, 12, 6, 7, 8, 9),
    (4, 5, 0, 1, 2, 3, 6, 7, 8, 9, 10, 11, 12),
    (7, 8, 4, 5, 6, 9, 10, 11, 12, 0, 1, 2, 3),
    (10, 11, 12, 7, 8, 9, 0, 1, 2, 3, 4, 5, 6),
)


def pack_kernel(sk_ref, w_ref, a_ref, wm_ref, wr_ref, am_ref, rows, last, rest):
    for k in range(2):
        for h in range(IRREPS):
            first = (k * IRREPS + h) * VH
            g = jnp.bitwise_xor(sk_ref[k], h)
            if k == 0:
                wm_ref[g, :, 0:VH] = w_ref[:, first : first + VH]
            else:
                wm_ref[g, :, VH:MAIN] = w_ref[:, first : first + MAIN - VH]
                wr_ref[:, h * 16 : (h + 1) * 16] = w_ref[:, first + MAIN - VH : first + VH]
    for half in range(2):
        rest[...] = jnp.zeros_like(rest)
        for i in range(HALF):
            first = (half * HALF + i) * VH
            rows[0:ROWS, 0:VH] = a_ref[0, :, first : first + VH].astype(F32)
            rows[0:ROWS, VH:COLS] = a_ref[1, :, first : first + VH].astype(F32)
            for lt in range(3):
                lanes = slice(lt * LANES, (lt + 1) * LANES)
                am_ref[half, lt * 25 + 3 * i : lt * 25 + 3 * i + 3] = (
                    rows[0:24, lanes].reshape(3, 8, LANES).astype(BF16)
                )
                last[lt, i : i + 1, :] = rows[24:25, lanes]
            rest[0:ROWS, i * 16 : (i + 1) * 16] = rows[0:ROWS, MAIN:COLS]
        for lt in range(3):
            am_ref[half, lt * 25 + 24] = last[lt].astype(BF16)
        am_ref[half, 75:79] = rest[...].reshape(4, 8, LANES).astype(BF16)


def pack(sk, w, a):
    vm = pl.BlockSpec(memory_space=pltpu.VMEM)
    return pl.pallas_call(
        pack_kernel,
        out_shape=(
            jax.ShapeDtypeStruct((IRREPS, COLS, MAIN), BF16),
            jax.ShapeDtypeStruct((COLS, LANES), BF16),
            jax.ShapeDtypeStruct((2, PIECES, 8, LANES), BF16),
        ),
        in_specs=[pl.BlockSpec(memory_space=pltpu.SMEM), vm, vm],
        out_specs=(vm, vm, vm),
        scratch_shapes=[
            pltpu.VMEM((32, 512), F32),
            pltpu.VMEM((3, 8, LANES), F32),
            pltpu.VMEM((32, LANES), F32),
        ],
        compiler_params=pltpu.CompilerParams(vmem_limit_bytes=40 << 20),
        name="pack",
    )(sk, w, a)


def is_value(y, value):
    return 1 - lax.div(lax.rem(y - value + RING, RING) + RING - 1, RING)


def main_kernel(
    s_ref, wm_ref, wr_ref, am_ref, d_ref, e_ref, o_ref,
    wb, wrb, ab, left, acc, snd,
    sib_send, sib_recv, own_sem, a_send, a_recv,
    w_send, w_recv, f_send, f_recv, o_send, o_recv,
):
    r = lax.axis_index("rep")
    col = lax.axis_index("tensor")
    q = lax.div(col, RING)
    y = lax.rem(col, RING)
    x, z = lax.div(q, 4), lax.rem(q, 4)
    phase = PAD * lax.rem(q, 2)
    sib = (1 - r, col)

    def plane_peer(o):
        px, pz = lax.rem(x + lax.div(o, 4), 4), lax.rem(z + lax.rem(o, 4), 4)
        return px * 4 + pz

    def ring_peer(d):
        return (r, q * RING + lax.rem(y + d, RING))

    barrier = pltpu.get_barrier_semaphore()

    def greet(o, c):
        pl.semaphore_signal(barrier, inc=1, device_id=(r, plane_peer(o) * RING + y), device_id_type=MESH)
        return c

    lax.fori_loop(1, PLANE, greet, 0)
    for d in (1, 2, 3):
        pl.semaphore_signal(barrier, inc=1, device_id=ring_peer(d), device_id_type=MESH)
    pl.semaphore_signal(barrier, inc=1, device_id=sib, device_id_type=MESH)
    pl.semaphore_wait(barrier, PLANE - 1 + 3 + 1)

    def remote(src, dst, ss, rs, dev):
        return pltpu.make_async_remote_copy(
            src_ref=src, dst_ref=dst, send_sem=ss, recv_sem=rs, device_id=dev, device_id_type=MESH
        )

    def w_rows(d):
        first = PAD + COLS * lax.rem(y + RING - d, RING)
        return pl.ds(pl.multiple_of(first, 16), COLS)

    def spot(d, half):
        lanes = pl.ds(pl.multiple_of(MAIN * half, LANES), MAIN)
        rest = pl.ds(pl.multiple_of(LANES * half, LANES), LANES)
        return wb.at[:, w_rows(d), lanes], wrb.at[w_rows(d), rest]

    def w_copies(d):
        dst, dst_r = spot(0, r)
        return (
            remote(wm_ref, dst, w_send.at[d, 0], w_recv.at[d, 0], ring_peer(d)),
            remote(wr_ref, dst_r, w_send.at[d, 1], w_recv.at[d, 1], ring_peer(d)),
        )

    def w_arrivals(d):
        dst, dst_r = spot(d, r)
        return (
            remote(wm_ref, dst, w_send.at[d, 0], w_recv.at[d, 0], ring_peer(d)),
            remote(wr_ref, dst_r, w_send.at[d, 1], w_recv.at[d, 1], ring_peer(d)),
        )

    def forwards(d, half):
        dst, dst_r = spot(d, half)
        src, src_r = (wm_ref, wr_ref) if d == 0 else (dst, dst_r)
        return (
            remote(src, dst, f_send.at[d, 0], f_recv.at[d, 0], sib),
            remote(src_r, dst_r, f_send.at[d, 1], f_recv.at[d, 1], sib),
        )

    a_sib = remote(am_ref.at[1 - r], ab.at[q, r], sib_send, sib_recv, sib)
    a_sib.start()
    a_own = pltpu.make_async_copy(am_ref.at[r], ab.at[q, r], own_sem.at[0])
    a_own.start()
    for d in (1, 3):
        for c in w_copies(d):
            c.start()
    for c in forwards(0, r):
        c.start()
    own_w, own_wr = spot(0, r)
    w_own = pltpu.make_async_copy(wm_ref, own_w, own_sem.at[1])
    w_own.start()
    wr_own = pltpu.make_async_copy(wr_ref, own_wr, own_sem.at[2])
    wr_own.start()
    a_own.wait()
    remote(am_ref.at[r], ab.at[q, 1 - r], sib_send, sib_recv, sib).wait_recv()

    def a_copy(o):
        return remote(ab.at[q], ab.at[q], a_send.at[o], a_recv.at[o], (r, plane_peer(o) * RING + y))

    def a_start(o, c):
        a_copy(o).start()
        return c

    lax.fori_loop(1, PLANE, a_start, 0)

    def a_wait(o, c):
        source = lax.rem(x + 4 - lax.div(o, 4), 4) * 4 + lax.rem(z + 4 - lax.rem(o, 4), 4)
        remote(ab.at[source], ab.at[source], a_send.at[o], a_recv.at[o], sib).wait_recv()
        return c

    lax.fori_loop(1, PLANE, a_wait, 0)

    lane_group = lax.div(lax.broadcasted_iota(jnp.int32, (BLOCK, LANES), 1), 16)

    def build(g, c):
        for i in range(HALF):
            h = jnp.bitwise_xor(g, s_ref[i])
            base = i * BLOCK
            for half in range(2):
                for lt in range(3):
                    lanes = slice(half * MAIN + lt * LANES, half * MAIN + (lt + 1) * LANES)
                    parts = [
                        ab[2 * h + zp, half, lt * 25 + 3 * i : lt * 25 + 3 * i + 3].astype(F32).reshape(24, LANES)
                        for zp in range(2)
                    ] + [ab[2 * h + zp, half, lt * 25 + 24].astype(F32) for zp in range(2)]
                    left[g, base : base + BLOCK, lanes] = jnp.concatenate(parts, axis=0).astype(BF16)
                tails = [ab[2 * h + zp, half, 75:79].astype(F32).reshape(32, LANES) for zp in range(2)]
                parts = [t[0:24] for t in tails] + [jnp.broadcast_to(t[24:25], (8, LANES)) for t in tails]
                tail = jnp.concatenate(parts, axis=0)
                place = jnp.bitwise_xor(g, s_ref[HALF + 2 * half + 1])
                tail = pltpu.roll(tail, lax.rem(16 * (place - i) + LANES, LANES), 1)
                tail = jnp.where(lane_group == place, tail, 0.0)
                lanes = slice(2 * MAIN + half * LANES, 2 * MAIN + (half + 1) * LANES)
                left[g, base : base + BLOCK, lanes] = tail.astype(BF16)
        return c

    lax.fori_loop(0, IRREPS, build, 0)
    w_own.wait()
    wr_own.wait()
    for c in forwards(0, 1 - r):
        c.wait_recv()

    lo, hi = 0, 0
    for value in range(RING):
        picked = is_value(y, value)
        lo = lo + picked * sum(ORDER[value][p] * 16**p for p in range(7))
        hi = hi + picked * sum(ORDER[value][p + 7] * 16**p for p in range(6))
    row_index = lax.broadcasted_iota(jnp.int32, (8, LANES), 0)
    NT = (((1,), (1,)), ((), ()))

    def out_copy(p, t, peer):
        lanes = pl.ds(pl.multiple_of(q * WIN + t * LANES, LANES), LANES)
        return snd.at[p, peer], o_ref.at[:, :, lanes]

    def step(p, carry):
        lo, hi = carry
        t = lax.rem(lo, 16)

        @pl.when(p == 2)
        def _():
            for d in (1, 3):
                for c in w_arrivals(d):
                    c.wait_recv()
                for c in forwards(d, r):
                    c.start()
            for d in (1, 3):
                for c in w_copies(d):
                    c.wait_send()
            for c in w_copies(2):
                c.start()
            for d in (1, 3):
                for c in forwards(d, 1 - r):
                    c.wait_recv()

        @pl.when(p == 9)
        def _():
            for c in w_arrivals(2):
                c.wait_recv()
            for c in forwards(2, r):
                c.start()
            for c in forwards(2, 1 - r):
                c.wait_recv()

        window = pl.ds(pl.multiple_of(t * LANES + PAD - phase, 16), LANES)

        def multiply(g, c):
            total = lax.dot_general(
                left[g, :, 0 : 2 * MAIN], wb[g, window, :], NT, preferred_element_type=F32
            )
            total = total + lax.dot_general(
                left[g, :, 2 * MAIN :], wrb[window, :], NT, preferred_element_type=F32
            )
            acc[g] = total.reshape(HALF, BLOCK, LANES)
            return c

        lax.fori_loop(0, IRREPS, multiply, 0)
        lanes = pl.ds(pl.multiple_of(t * LANES, LANES), LANES)

        def finish(s, c):
            h = 2 * lax.rem(x + lax.div(s, 2), 4) + lax.rem(lax.div(z, 2) + s, 2)
            energy_a = e_ref[h]
            tail = [jnp.zeros((8, LANES), F32), jnp.zeros((8, LANES), F32)]
            for i in range(HALF):
                g = jnp.bitwise_xor(h, s_ref[i])
                den = d_ref[h, i : i + 1, lanes] - energy_a
                value = acc[g, i] / den
                for zp in range(2):
                    snd[p, 2 * h + zp, 3 * i : 3 * i + 3] = (
                        value[24 * zp : 24 * zp + 24].reshape(3, 8, LANES).astype(BF16)
                    )
                    tail[zp] = jnp.where(row_index == i, value[48 + 8 * zp : 56 + 8 * zp], tail[zp])
            for zp in range(2):
                peer = 2 * h + zp
                snd[p, peer, 24] = tail[zp].astype(BF16)
                src, dst = out_copy(p, t, peer)

                @pl.when(peer != q)
                def _():
                    remote(src, dst, o_send.at[peer], o_recv.at[q], (r, peer * RING + y)).start()

                @pl.when(peer == q)
                def _():
                    pltpu.make_async_copy(src, dst, o_send.at[peer]).start()

            return c

        lax.fori_loop(0, IRREPS, finish, 0)
        return lax.div(lo, 16) + lax.rem(hi, 16) * 16**6, lax.div(hi, 16)

    lax.fori_loop(0, TILES, step, (lo, hi))

    a_sib.wait_send()
    for d in range(RING):
        for c in forwards(d, r):
            c.wait_send()
    for c in w_copies(2):
        c.wait_send()

    def drain(o, c):
        a_copy(o).wait_send()
        return c

    lax.fori_loop(1, PLANE, drain, 0)

    def all_tiles(peer):
        lanes = pl.ds(pl.multiple_of(peer * WIN, LANES), WIN)
        return o_ref.at[:, :, lanes]

    def drain_out(o, c):
        peer = plane_peer(o)
        whole = all_tiles(peer)
        remote(whole, whole, o_send.at[peer], o_recv.at[peer], sib).wait_send()
        remote(whole, whole, o_send.at[peer], o_recv.at[peer], sib).wait_recv()
        return c

    lax.fori_loop(1, PLANE, drain_out, 0)
    own = all_tiles(q)
    pltpu.make_async_copy(own, own, o_send.at[q]).wait()


def exchange(symmetry, wm, wr, am, d_table, e_table):
    vm = pl.BlockSpec(memory_space=pltpu.VMEM)
    hbm = pl.BlockSpec(memory_space=pl.ANY)
    dma = pltpu.SemaphoreType.DMA
    return pl.pallas_call(
        main_kernel,
        out_shape=jax.ShapeDtypeStruct((25, 8, PLANE * WIN), BF16),
        in_specs=[pl.BlockSpec(memory_space=pltpu.SMEM), hbm, hbm, hbm, vm, vm],
        out_specs=hbm,
        scratch_shapes=[
            pltpu.VMEM((IRREPS, RING * COLS + 2 * PAD, 2 * MAIN), BF16),
            pltpu.VMEM((RING * COLS + 2 * PAD, 2 * LANES), BF16),
            pltpu.VMEM((PLANE, 2, PIECES, 8, LANES), BF16),
            pltpu.VMEM((IRREPS, HALF * BLOCK, 2 * MAIN + 2 * LANES), BF16),
            pltpu.VMEM((IRREPS, HALF, BLOCK, LANES), F32),
            pltpu.VMEM((TILES, PLANE, 25, 8, LANES), BF16),
            dma, dma, dma((3,)), dma((PLANE,)), dma((PLANE,)),
            dma((RING, 2)), dma((RING, 2)), dma((RING, 2)), dma((RING, 2)),
            dma((PLANE,)), dma((PLANE,)),
        ],
        compiler_params=pltpu.CompilerParams(
            collective_id=0, has_side_effects=True, vmem_limit_bytes=60 << 20
        ),
        name="exchange",
    )(symmetry, wm, wr, am, d_table, e_table)


def unpack_kernel(o_ref, out_ref):
    lane = lax.broadcasted_iota(jnp.int32, (24, LANES), 1)
    cut = 12 * LANES

    def joined(v):
        middle = jnp.where(lane[: v.shape[0]] < PAD, v[:, cut:WIN], v[:, WIN : WIN + LANES])
        return v[:, :cut], middle, v[:, WIN + LANES :]

    for i in range(HALF):
        v = o_ref[3 * i : 3 * i + 3].astype(F32).reshape(24, 2 * WIN)
        start, middle, end = joined(v)
        out_ref[i, 0:24, 0:cut] = start.astype(BF16)
        out_ref[i, 0:24, cut:WIN] = middle.astype(BF16)
        out_ref[i, 0:24, WIN:] = end.astype(BF16)
        start, middle, end = joined(o_ref[24].astype(F32)[i : i + 1])
        out_ref[i, 24:25, 0:cut] = start.astype(BF16)
        out_ref[i, 24:25, cut:WIN] = middle.astype(BF16)
        out_ref[i, 24:25, WIN:] = end.astype(BF16)


def unpack(o):
    width = 2 * RING * COLS
    return pl.pallas_call(
        unpack_kernel,
        grid=(PLANE // 2,),
        out_shape=jax.ShapeDtypeStruct((HALF, ROWS, width * PLANE // 2), BF16),
        in_specs=[pl.BlockSpec((25, 8, 2 * WIN), lambda n: (0, 0, n))],
        out_specs=pl.BlockSpec((HALF, ROWS, width), lambda n: (0, 0, n)),
        compiler_params=pltpu.CompilerParams(vmem_limit_bytes=40 << 20),
        name="unpack",
    )(o)


def per_device(
    amplitudes, intermediate, occ_irrep, i_window, j_window, k_window, occ_energy, virt_energy
):
    r = lax.axis_index("rep")
    col = lax.axis_index("tensor")
    q = col // RING
    sym_k = occ_irrep[k_window]
    own_i = lax.dynamic_slice_in_dim(i_window, r * HALF, HALF)
    own_j = lax.dynamic_slice_in_dim(j_window, q * 2 * RING, 2 * RING)
    sym_i, sym_j = occ_irrep[own_i], occ_irrep[own_j]
    wm, wr, am = pack(
        lax.dynamic_slice_in_dim(sym_k, 2 * r, 2), intermediate.reshape(COLS, -1), amplitudes
    )
    irreps = jnp.arange(IRREPS, dtype=jnp.int32)
    table = virt_energy.reshape(IRREPS, VH)
    label = irreps[:, None, None] ^ sym_i[None, :, None] ^ sym_j[None, None, :]
    energy_b = jnp.zeros(label.shape + (VH,), F32)
    for value in range(IRREPS):
        energy_b = jnp.where(label[..., None] == value, table[value], energy_b)
    d_table = occ_energy[own_i][None, :, None, None] + occ_energy[own_j][None, None, :, None] - energy_b
    d_table = d_table.reshape(IRREPS, HALF, RING * COLS)
    ones = jnp.ones((IRREPS, HALF, PAD), F32)
    d_table = jnp.where(
        q % 2 == 0,
        jnp.concatenate([d_table, ones], axis=2),
        jnp.concatenate([ones, d_table], axis=2),
    )
    pairs = lax.dynamic_index_in_dim(virt_energy.reshape(IRREPS, 2, RING, ROWS), col % RING, 2, keepdims=False)
    e_rows = jnp.concatenate(
        [
            pairs[:, 0, :24], pairs[:, 1, :24],
            jnp.broadcast_to(pairs[:, 0, 24:], (IRREPS, 8)),
            jnp.broadcast_to(pairs[:, 1, 24:], (IRREPS, 8)),
        ],
        axis=1,
    )
    e_table = jnp.broadcast_to(e_rows[:, :, None], (IRREPS, BLOCK, LANES))
    o = exchange(jnp.concatenate([sym_i, sym_k]), wm, wr, am, d_table, e_table)
    return unpack(o)


def solution(mesh):
    return jax.shard_map(
        per_device,
        mesh=mesh,
        in_specs=(P("rep", "tensor", None), P("tensor", None, "rep"), P(), P(), P(), P(), P(), P()),
        out_specs=P("rep", "tensor", None),
        check_vma=False,
    )
```

```python
import functools
import jax
import jax.numpy as jnp
from jax import lax
from jax.experimental import pallas as pl
from jax.experimental.pallas import tpu as pltpu
from jax.sharding import PartitionSpec as P

IRREPS = 8
VH = 200
ROWS = 25
HALF = 8
PLANE = 16
RING = 4
COLS = 400
LANES = 128
MAIN = 384
TILES = 13
WIN = TILES * LANES
PIECES = 79
PAD = 64
BLOCK = 64
MESH = pl.DeviceIdType.MESH
F32 = jnp.float32
BF16 = jnp.bfloat16
ORDER = (
    (0, 1, 2, 3, 4, 5, 10, 11, 12, 6, 7, 8, 9),
    (4, 5, 0, 1, 2, 3, 6, 7, 8, 9, 10, 11, 12),
    (7, 8, 4, 5, 6, 9, 10, 11, 12, 0, 1, 2, 3),
    (10, 11, 12, 7, 8, 9, 0, 1, 2, 3, 4, 5, 6),
)


def pack_kernel(
    irrep_ref, k_ref, w_ref, a_ref, wm_ref, wr_ref, am_ref, wm, wr, am, rows, last, rest, sem
):
    r = lax.axis_index("rep")
    for k in range(2):
        label = irrep_ref[k_ref[2 * r + k]]
        for h in range(IRREPS):
            first = (k * IRREPS + h) * VH
            g = jnp.bitwise_xor(label, h)
            if k == 0:
                wm[g, :, 0:VH] = w_ref[:, first : first + VH]
            else:
                wm[g, :, VH:MAIN] = w_ref[:, first : first + MAIN - VH]
                wr[:, h * 16 : (h + 1) * 16] = w_ref[:, first + MAIN - VH : first + VH]
    copies = [
        pltpu.make_async_copy(wm, wm_ref, sem.at[0]),
        pltpu.make_async_copy(wr, wr_ref, sem.at[1]),
        pltpu.make_async_copy(am, am_ref, sem.at[2]),
    ]
    copies[0].start()
    copies[1].start()
    for half in range(2):
        rest[...] = jnp.zeros_like(rest)
        for i in range(HALF):
            first = (half * HALF + i) * VH
            rows[0:ROWS, 0:VH] = a_ref[0, :, first : first + VH].astype(F32)
            rows[0:ROWS, VH:COLS] = a_ref[1, :, first : first + VH].astype(F32)
            for lt in range(3):
                lanes = slice(lt * LANES, (lt + 1) * LANES)
                am[half, lt * 25 + 3 * i : lt * 25 + 3 * i + 3] = (
                    rows[0:24, lanes].reshape(3, 8, LANES).astype(BF16)
                )
                last[lt, i : i + 1, :] = rows[24:25, lanes]
            rest[0:ROWS, i * 16 : (i + 1) * 16] = rows[0:ROWS, MAIN:COLS]
        for lt in range(3):
            am[half, lt * 25 + 24] = last[lt].astype(BF16)
        am[half, 75:79] = rest[...].reshape(4, 8, LANES).astype(BF16)
    copies[2].start()
    for c in copies:
        c.wait()


def pack(irrep, k, w, a):
    vm = pl.BlockSpec(memory_space=pltpu.VMEM)
    sm = pl.BlockSpec(memory_space=pltpu.SMEM)
    hbm = pl.BlockSpec(memory_space=pl.ANY)
    shapes = ((IRREPS, COLS, MAIN), (COLS, LANES), (2, PIECES, 8, LANES))
    return pl.pallas_call(
        pack_kernel,
        out_shape=tuple(jax.ShapeDtypeStruct(shape, BF16) for shape in shapes),
        in_specs=[sm, sm, vm, vm],
        out_specs=(hbm, hbm, hbm),
        scratch_shapes=[
            *(pltpu.VMEM(shape, BF16) for shape in shapes),
            pltpu.VMEM((32, 512), F32),
            pltpu.VMEM((3, 8, LANES), F32),
            pltpu.VMEM((32, LANES), F32),
            pltpu.SemaphoreType.DMA((3,)),
        ],
        compiler_params=pltpu.CompilerParams(vmem_limit_bytes=58 << 20),
        name="pack",
    )(irrep, k, w, a)


def is_value(y, value):
    return 1 - lax.div(lax.rem(y - value + RING, RING) + RING - 1, RING)


def main_kernel(
    irrep_ref, i_ref, j_ref, k_ref, occ_ref, virt_ref, table_ref, wm_ref, wr_ref, am_ref, o_ref,
    wb, wrb, ab, left, acc, snd, dtab,
    sib_send, sib_recv, own_sem, a_send, a_recv,
    w_send, w_recv, h_send, h_recv, f_send, f_recv, o_send, o_recv,
):
    r = lax.axis_index("rep")
    col = lax.axis_index("tensor")
    q = lax.div(col, RING)
    y = lax.rem(col, RING)
    x, z = lax.div(q, 4), lax.rem(q, 4)
    phase = PAD * lax.rem(q, 2)
    sib = (1 - r, col)

    def plane_peer(o):
        px, pz = lax.rem(x + lax.div(o, 4), 4), lax.rem(z + lax.rem(o, 4), 4)
        return px * 4 + pz

    def ring_peer(d):
        return (r, q * RING + lax.rem(y + d, RING))

    barrier = pltpu.get_barrier_semaphore()

    def greet(o, c):
        pl.semaphore_signal(barrier, inc=1, device_id=(r, plane_peer(o) * RING + y), device_id_type=MESH)
        return c

    lax.fori_loop(1, PLANE, greet, 0)
    for d in (1, 3):
        pl.semaphore_signal(barrier, inc=1, device_id=ring_peer(d), device_id_type=MESH)
    pl.semaphore_signal(barrier, inc=1, device_id=sib, device_id_type=MESH)
    pl.semaphore_wait(barrier, PLANE - 1 + 2 + 1)

    def remote(src, dst, ss, rs, dev):
        return pltpu.make_async_remote_copy(
            src_ref=src, dst_ref=dst, send_sem=ss, recv_sem=rs, device_id=dev, device_id_type=MESH
        )

    def w_rows(d):
        first = PAD + COLS * lax.rem(y + RING - d, RING)
        return pl.ds(pl.multiple_of(first, 16), COLS)

    def spot(d, half):
        lanes = pl.ds(pl.multiple_of(MAIN * half, LANES), MAIN)
        rest = pl.ds(pl.multiple_of(LANES * half, LANES), LANES)
        return wb.at[:, w_rows(d), lanes], wrb.at[w_rows(d), rest]

    def w_copies(d):
        dst, dst_r = spot(0, r)
        return (
            remote(wm_ref, dst, w_send.at[d, 0], w_recv.at[d, 0], ring_peer(d)),
            remote(wr_ref, dst_r, w_send.at[d, 1], w_recv.at[d, 1], ring_peer(d)),
        )

    def w_arrivals(d):
        dst, dst_r = spot(d, r)
        return (
            remote(wm_ref, dst, w_send.at[d, 0], w_recv.at[d, 0], ring_peer(d)),
            remote(wr_ref, dst_r, w_send.at[d, 1], w_recv.at[d, 1], ring_peer(d)),
        )

    def forwards(d, half):
        dst, dst_r = spot(d, half)
        src, src_r = (wm_ref, wr_ref) if d == 0 else (dst, dst_r)
        return (
            remote(src, dst, f_send.at[d, 0], f_recv.at[d, 0], sib),
            remote(src_r, dst_r, f_send.at[d, 1], f_recv.at[d, 1], sib),
        )

    def far_copies():
        out = []
        for n, (came, to) in enumerate(((1, 1), (3, 3))):
            blocks = slice(4 * n, 4 * n + 4)
            lanes = pl.ds(pl.multiple_of(MAIN * r, LANES), MAIN)
            part = wb.at[blocks, w_rows(came), lanes]
            out.append(remote(part, part, h_send.at[n], h_recv.at[n], ring_peer(to)))
        part = wrb.at[w_rows(1), pl.ds(pl.multiple_of(LANES * r, LANES), LANES)]
        out.append(remote(part, part, h_send.at[2], h_recv.at[2], ring_peer(1)))
        return out

    def far_arrivals():
        out = []
        for n in range(2):
            lanes = pl.ds(pl.multiple_of(MAIN * r, LANES), MAIN)
            part = wb.at[4 * n : 4 * n + 4, w_rows(2), lanes]
            out.append(remote(part, part, h_send.at[n], h_recv.at[n], sib))
        part = wrb.at[w_rows(2), pl.ds(pl.multiple_of(LANES * r, LANES), LANES)]
        out.append(remote(part, part, h_send.at[2], h_recv.at[2], sib))
        return out

    a_sib = remote(am_ref.at[1 - r], ab.at[x, z, r], sib_send, sib_recv, sib)
    a_sib.start()
    a_own = pltpu.make_async_copy(am_ref.at[r], ab.at[x, z, r], own_sem.at[0])
    a_own.start()
    for d in (1, 3):
        for c in w_copies(d):
            c.start()
    for c in forwards(0, r):
        c.start()
    own_w, own_wr = spot(0, r)
    w_own = pltpu.make_async_copy(wm_ref, own_w, own_sem.at[1])
    w_own.start()
    wr_own = pltpu.make_async_copy(wr_ref, own_wr, own_sem.at[2])
    wr_own.start()
    a_own.wait()
    remote(am_ref.at[r], ab.at[x, z, 1 - r], sib_send, sib_recv, sib).wait_recv()

    def x_peer(d):
        return (r, (lax.rem(x + d, 4) * 4 + z) * RING + y)

    def z_peer(d):
        return (r, (x * 4 + lax.rem(z + d, 4)) * RING + y)

    def a_first(n, d, back):
        sx, sz = lax.rem(x + 4 - back, 4), lax.rem(z + 4 - back, 4)
        part = ab.at[sx, z, 0] if n == 0 else ab.at[x, sz, 1]
        return remote(part, part, a_send.at[0, n, d], a_recv.at[0, n, d], x_peer(d) if n == 0 else z_peer(d))

    def a_second(n, d, back):
        sx, sz = lax.rem(x + 4 - back, 4), lax.rem(z + 4 - back, 4)
        part = ab.at[:, sz, 0] if n == 0 else ab.at[sx, :, 1]
        return remote(part, part, a_send.at[1, n, d], a_recv.at[1, n, d], z_peer(d) if n == 0 else x_peer(d))

    for d in (1, 3, 2):
        for n in range(2):
            a_first(n, d, 0).start()
    for n in range(2):
        for d in (1, 3, 2):
            a_first(n, d, d).wait_recv()
        for d in (1, 3, 2):
            a_second(n, d, 0).start()

    def energies(h, c):
        for j in range(2 * RING):
            orbital_j = j_ref[q * 2 * RING + j]
            for i in range(HALF):
                orbital_i = i_ref[r * HALF + i]
                label = jnp.bitwise_xor(jnp.bitwise_xor(h, irrep_ref[orbital_i]), irrep_ref[orbital_j])
                energy = occ_ref[orbital_i] + occ_ref[orbital_j]
                dtab[h, i : i + 1, j * VH : (j + 1) * VH] = energy - table_ref[label]
        dtab[h, :, RING * COLS :] = jnp.ones((HALF, PAD), F32)
        dtab[h] = pltpu.roll(dtab[h], phase, 1)
        return c

    lax.fori_loop(0, IRREPS, energies, 0)
    for n in range(2):
        for d in (1, 3, 2):
            a_second(n, d, d).wait_recv()

    lane_group = lax.div(lax.broadcasted_iota(jnp.int32, (BLOCK, LANES), 1), 16)

    def build(g, c):
        for i in range(HALF):
            h = jnp.bitwise_xor(g, irrep_ref[i_ref[r * HALF + i]])
            hx, hz = lax.div(h, 2), 2 * lax.rem(h, 2)
            base = i * BLOCK
            for half in range(2):
                for lt in range(3):
                    lanes = slice(half * MAIN + lt * LANES, half * MAIN + (lt + 1) * LANES)
                    parts = [
                        ab[hx, hz + zp, half, lt * 25 + 3 * i : lt * 25 + 3 * i + 3].astype(F32).reshape(24, LANES)
                        for zp in range(2)
                    ] + [ab[hx, hz + zp, half, lt * 25 + 24].astype(F32) for zp in range(2)]
                    left[g, base : base + BLOCK, lanes] = jnp.concatenate(parts, axis=0).astype(BF16)
                tails = [ab[hx, hz + zp, half, 75:79].astype(F32).reshape(32, LANES) for zp in range(2)]
                parts = [t[0:24] for t in tails] + [jnp.broadcast_to(t[24:25], (8, LANES)) for t in tails]
                tail = jnp.concatenate(parts, axis=0)
                place = jnp.bitwise_xor(g, irrep_ref[k_ref[2 * half + 1]])
                tail = pltpu.roll(tail, lax.rem(16 * (place - i) + LANES, LANES), 1)
                tail = jnp.where(lane_group == place, tail, 0.0)
                lanes = slice(2 * MAIN + half * LANES, 2 * MAIN + (half + 1) * LANES)
                left[g, base : base + BLOCK, lanes] = tail.astype(BF16)
        return c

    lax.fori_loop(0, IRREPS, build, 0)
    w_own.wait()
    wr_own.wait()
    for c in forwards(0, 1 - r):
        c.wait_recv()

    lo, hi = 0, 0
    for value in range(RING):
        picked = is_value(y, value)
        lo = lo + picked * sum(ORDER[value][p] * 16**p for p in range(7))
        hi = hi + picked * sum(ORDER[value][p + 7] * 16**p for p in range(6))
    row_index = lax.broadcasted_iota(jnp.int32, (8, LANES), 0)
    NT = (((1,), (1,)), ((), ()))

    def out_copy(p, t, peer):
        return snd.at[p, peer], o_ref.at[q * TILES + t]

    def step(p, carry):
        lo, hi = carry
        t = lax.rem(lo, 16)

        @pl.when(p == 2)
        def _():
            for d in (1, 3):
                for c in w_arrivals(d):
                    c.wait_recv()
            for c in far_copies():
                c.start()
            for d in (1, 3):
                for c in forwards(d, r):
                    c.start()
            for d in (1, 3):
                for c in forwards(d, 1 - r):
                    c.wait_recv()

        @pl.when(p == 9)
        def _():
            for c in far_arrivals():
                c.wait_recv()
            for c in forwards(2, r):
                c.start()
            for c in forwards(2, 1 - r):
                c.wait_recv()

        window = pl.ds(pl.multiple_of(t * LANES + PAD - phase, 16), LANES)

        def multiply(g, c):
            total = lax.dot_general(
                left[g, :, 0 : 2 * MAIN], wb[g, window, :], NT, preferred_element_type=F32
            )
            total = total + lax.dot_general(
                left[g, :, 2 * MAIN :], wrb[window, :], NT, preferred_element_type=F32
            )
            acc[g] = total.reshape(HALF, BLOCK, LANES)
            return c

        lax.fori_loop(0, IRREPS, multiply, 0)
        lanes = pl.ds(pl.multiple_of(t * LANES, LANES), LANES)

        def finish(s, c):
            h = 2 * lax.rem(x + lax.div(s, 2), 4) + lax.rem(lax.div(z, 2) + s, 2)
            values = [acc[jnp.bitwise_xor(h, irrep_ref[i_ref[r * HALF + i]]), i] for i in range(HALF)]
            energy = dtab[h, :, lanes]
            for zp in range(2):
                first = ROWS * (8 * h + 4 * zp + y)
                last = jnp.zeros((8, LANES), F32)
                for i in range(HALF):
                    last = jnp.where(row_index == i, values[i][48 + 8 * zp : 56 + 8 * zp], last)
                snd[p, 2 * h + zp, 24] = (last / (energy - virt_ref[first + 24])).astype(BF16)
                for n in range(3):
                    top = 24 * zp + 8 * n
                    tiles = jnp.stack([v[top : top + 8] for v in values]).transpose(1, 0, 2)
                    for m in range(8):
                        value = tiles[m] / (energy - virt_ref[first + 8 * n + m])
                        snd[p, 2 * h + zp, 8 * n + m] = value.astype(BF16)
            for zp in range(2):
                peer = 2 * h + zp
                src, dst = out_copy(p, t, peer)

                @pl.when(peer != q)
                def _():
                    remote(src, dst, o_send.at[peer], o_recv.at[q], (r, peer * RING + y)).start()

                @pl.when(peer == q)
                def _():
                    pltpu.make_async_copy(src, dst, o_send.at[peer]).start()

            return c

        lax.fori_loop(0, IRREPS, finish, 0)
        return lax.div(lo, 16) + lax.rem(hi, 16) * 16**6, lax.div(hi, 16)

    lax.fori_loop(0, TILES, step, (lo, hi))

    a_sib.wait_send()
    for d in range(RING):
        for c in forwards(d, r):
            c.wait_send()
    for d in (1, 3):
        for c in w_copies(d):
            c.wait_send()
    for c in far_copies():
        c.wait_send()
    for n in range(2):
        for d in (1, 3, 2):
            a_first(n, d, 0).wait_send()
            a_second(n, d, 0).wait_send()

    def all_tiles(peer):
        return o_ref.at[pl.ds(peer * TILES, TILES)]

    def drain_out(o, c):
        peer = plane_peer(o)
        whole = all_tiles(peer)
        remote(whole, whole, o_send.at[peer], o_recv.at[peer], sib).wait_send()
        remote(whole, whole, o_send.at[peer], o_recv.at[peer], sib).wait_recv()
        return c

    lax.fori_loop(1, PLANE, drain_out, 0)
    own = all_tiles(q)
    pltpu.make_async_copy(own, own, o_send.at[q]).wait()


def exchange(irrep, i, j, k, occ, virt, wm, wr, am):
    vm = pl.BlockSpec(memory_space=pltpu.VMEM)
    sm = pl.BlockSpec(memory_space=pltpu.SMEM)
    hbm = pl.BlockSpec(memory_space=pl.ANY)
    dma = pltpu.SemaphoreType.DMA
    return pl.pallas_call(
        main_kernel,
        out_shape=jax.ShapeDtypeStruct((PLANE * TILES, ROWS, 8, LANES), BF16),
        in_specs=[sm, sm, sm, sm, sm, sm, vm, hbm, hbm, hbm],
        out_specs=hbm,
        scratch_shapes=[
            pltpu.VMEM((IRREPS, RING * COLS + 2 * PAD, 2 * MAIN), BF16),
            pltpu.VMEM((RING * COLS + 2 * PAD, 2 * LANES), BF16),
            pltpu.VMEM((4, 4, 2, PIECES, 8, LANES), BF16),
            pltpu.VMEM((IRREPS, HALF * BLOCK, 2 * MAIN + 2 * LANES), BF16),
            pltpu.VMEM((IRREPS, HALF, BLOCK, LANES), F32),
            pltpu.VMEM((TILES, PLANE, ROWS, 8, LANES), BF16),
            pltpu.VMEM((IRREPS, HALF, WIN), F32),
            dma, dma, dma((3,)), dma((2, 2, 4)), dma((2, 2, 4)),
            dma((RING, 2)), dma((RING, 2)), dma((3,)), dma((3,)), dma((RING, 2)), dma((RING, 2)),
            dma((PLANE,)), dma((PLANE,)),
        ],
        compiler_params=pltpu.CompilerParams(
            collective_id=0, has_side_effects=True, vmem_limit_bytes=60 << 20
        ),
        name="exchange",
    )(irrep, i, j, k, occ, virt, virt.reshape(IRREPS, 1, VH), wm, wr, am)


def unpack_kernel(o_ref, out_ref):
    low = lax.broadcasted_iota(jnp.int32, (ROWS, 8, LANES), 2) < PAD
    for t in range(TILES - 1):
        out_ref[:, :, t * LANES : (t + 1) * LANES] = o_ref[t]
        out_ref[:, :, (t + TILES) * LANES : (t + TILES + 1) * LANES] = o_ref[t + TILES + 1]
    middle = jnp.where(low, o_ref[TILES - 1].astype(F32), o_ref[TILES].astype(F32))
    out_ref[:, :, WIN - LANES : WIN] = middle.astype(BF16)


def unpack(o):
    width = 2 * RING * COLS
    return pl.pallas_call(
        unpack_kernel,
        grid=(PLANE // 2,),
        out_shape=jax.ShapeDtypeStruct((ROWS, HALF, width * PLANE // 2), BF16),
        in_specs=[pl.BlockSpec((2 * TILES, ROWS, 8, LANES), lambda n: (n, 0, 0, 0))],
        out_specs=pl.BlockSpec((ROWS, HALF, width), lambda n: (0, 0, n)),
        compiler_params=pltpu.CompilerParams(vmem_limit_bytes=58 << 20),
        name="unpack",
    )(o)


def per_device(
    amplitudes, intermediate, occ_irrep, i_window, j_window, k_window, occ_energy, virt_energy
):
    wm, wr, am = pack(occ_irrep, k_window, intermediate.reshape(COLS, -1), amplitudes)
    o = exchange(
        occ_irrep, i_window, j_window, k_window, occ_energy, virt_energy, wm, wr, am
    )
    return unpack(o).transpose(1, 0, 2)


def solution(mesh):
    return jax.shard_map(
        per_device,
        mesh=mesh,
        in_specs=(P("rep", "tensor", None), P("tensor", None, "rep"), P(), P(), P(), P(), P(), P()),
        out_specs=P("rep", "tensor", None),
        check_vma=False,
    )
```

```python
import functools
import jax
import jax.numpy as jnp
from jax import lax
from jax.experimental import pallas as pl
from jax.experimental.pallas import tpu as pltpu
from jax.sharding import PartitionSpec as P

IRREPS = 8
VH = 200
ROWS = 25
HALF = 8
PLANE = 16
RING = 4
COLS = 400
LANES = 128
MAIN = 384
TILES = 13
WIN = TILES * LANES
PIECES = 79
PAD = 64
BLOCK = 64
MESH = pl.DeviceIdType.MESH
F32 = jnp.float32
BF16 = jnp.bfloat16
ORDER = (
    (0, 1, 2, 3, 4, 11, 12, 5, 10, 6, 7, 8, 9),
    (4, 5, 3, 2, 6, 7, 0, 1, 8, 9, 10, 11, 12),
    (7, 8, 6, 5, 9, 10, 4, 11, 12, 0, 1, 2, 3),
    (10, 11, 12, 9, 8, 0, 1, 7, 2, 3, 4, 5, 6),
)
PARTS = {1: ((144, 256), (0, 144)), 3: ((0, 256), (256, 144))}
SENDS = (
    (2, 2), (2, 1), (1, 2), (2, 3), (3, 2), (1, 1), (3, 3), (1, 3),
    (3, 1), (2, 0), (0, 2), (1, 0), (0, 1), (3, 0), (0, 3),
)


def pack_kernel(
    irrep_ref, k_ref, w_ref, a_ref, wm_ref, wr_ref, am_ref, wm, wr, am, rows, last, rest, sem
):
    r = lax.axis_index("rep")
    for k in range(2):
        label = irrep_ref[k_ref[2 * r + k]]
        for h in range(IRREPS):
            first = (k * IRREPS + h) * VH
            g = jnp.bitwise_xor(label, h)
            if k == 0:
                wm[g, :, 0:VH] = w_ref[:, first : first + VH]
            else:
                wm[g, :, VH:MAIN] = w_ref[:, first : first + MAIN - VH]
                wr[:, h * 16 : (h + 1) * 16] = w_ref[:, first + MAIN - VH : first + VH]
    copies = [
        pltpu.make_async_copy(wm, wm_ref, sem.at[0]),
        pltpu.make_async_copy(wr, wr_ref, sem.at[1]),
        pltpu.make_async_copy(am, am_ref, sem.at[2]),
    ]
    copies[0].start()
    copies[1].start()
    for half in range(2):
        rest[...] = jnp.zeros_like(rest)
        for i in range(HALF):
            first = (half * HALF + i) * VH
            rows[0:ROWS, 0:VH] = a_ref[0, :, first : first + VH].astype(F32)
            rows[0:ROWS, VH:COLS] = a_ref[1, :, first : first + VH].astype(F32)
            for lt in range(3):
                lanes = slice(lt * LANES, (lt + 1) * LANES)
                am[half, lt * 25 + 3 * i : lt * 25 + 3 * i + 3] = (
                    rows[0:24, lanes].reshape(3, 8, LANES).astype(BF16)
                )
                last[lt, i : i + 1, :] = rows[24:25, lanes]
            rest[0:ROWS, i * 16 : (i + 1) * 16] = rows[0:ROWS, MAIN:COLS]
        for lt in range(3):
            am[half, lt * 25 + 24] = last[lt].astype(BF16)
        am[half, 75:79] = rest[...].reshape(4, 8, LANES).astype(BF16)
    copies[2].start()
    for c in copies:
        c.wait()


def pack(irrep, k, w, a):
    vm = pl.BlockSpec(memory_space=pltpu.VMEM)
    sm = pl.BlockSpec(memory_space=pltpu.SMEM)
    hbm = pl.BlockSpec(memory_space=pl.ANY)
    shapes = ((IRREPS, COLS, MAIN), (COLS, LANES), (2, PIECES, 8, LANES))
    return pl.pallas_call(
        pack_kernel,
        out_shape=tuple(jax.ShapeDtypeStruct(shape, BF16) for shape in shapes),
        in_specs=[sm, sm, vm, vm],
        out_specs=(hbm, hbm, hbm),
        scratch_shapes=[
            *(pltpu.VMEM(shape, BF16) for shape in shapes),
            pltpu.VMEM((32, 512), F32),
            pltpu.VMEM((3, 8, LANES), F32),
            pltpu.VMEM((32, LANES), F32),
            pltpu.SemaphoreType.DMA((3,)),
        ],
        compiler_params=pltpu.CompilerParams(vmem_limit_bytes=58 << 20),
        name="pack",
    )(irrep, k, w, a)


def is_value(y, value):
    return 1 - lax.div(lax.rem(y - value + RING, RING) + RING - 1, RING)


def main_kernel(
    irrep_ref, i_ref, j_ref, k_ref, occ_ref, virt_ref, table_ref, wm_ref, wr_ref, am_ref, o_ref,
    wb, wrb, ab, left, acc, snd, dtab,
    sib_send, sib_recv, own_sem, a_send, a_recv,
    w_send, w_recv, h_send, h_recv, f_send, f_recv, o_send, o_recv,
):
    r = lax.axis_index("rep")
    col = lax.axis_index("tensor")
    q = lax.div(col, RING)
    y = lax.rem(col, RING)
    x, z = lax.div(q, 4), lax.rem(q, 4)
    phase = PAD * lax.rem(q, 2)
    sib = (1 - r, col)

    def plane_peer(o):
        px, pz = lax.rem(x + lax.div(o, 4), 4), lax.rem(z + lax.rem(o, 4), 4)
        return px * 4 + pz

    def ring_peer(d):
        return (r, q * RING + lax.rem(y + d, RING))

    barrier = pltpu.get_barrier_semaphore()

    def greet(o, c):
        pl.semaphore_signal(barrier, inc=1, device_id=(r, plane_peer(o) * RING + y), device_id_type=MESH)
        return c

    lax.fori_loop(1, PLANE, greet, 0)
    for d in (1, 3):
        pl.semaphore_signal(barrier, inc=1, device_id=ring_peer(d), device_id_type=MESH)
    pl.semaphore_signal(barrier, inc=1, device_id=sib, device_id_type=MESH)
    pl.semaphore_wait(barrier, PLANE - 1 + 2 + 1)

    def remote(src, dst, ss, rs, dev):
        return pltpu.make_async_remote_copy(
            src_ref=src, dst_ref=dst, send_sem=ss, recv_sem=rs, device_id=dev, device_id_type=MESH
        )

    def spot(back, half, first=0, size=COLS):
        top = PAD + COLS * lax.rem(y + RING - back, RING) + first
        rows = pl.ds(pl.multiple_of(top, 16), size)
        lanes = pl.ds(pl.multiple_of(MAIN * half, LANES), MAIN)
        rest = pl.ds(pl.multiple_of(LANES * half, LANES), LANES)
        return wb.at[:, rows, lanes], wrb.at[rows, rest]

    def w_copies(d, part, back):
        first, size = PARTS[d][part]
        rows = pl.ds(first, size)
        dst, dst_r = spot(back, r, first, size)
        return (
            remote(wm_ref.at[:, rows], dst, w_send.at[d, part, 0], w_recv.at[d, part, 0], ring_peer(d)),
            remote(wr_ref.at[rows], dst_r, w_send.at[d, part, 1], w_recv.at[d, part, 1], ring_peer(d)),
        )

    def forwards(d, half, part=0):
        first, size = PARTS[d][part] if d in PARTS else (0, COLS)
        dst, dst_r = spot(d, half, first, size)
        src, src_r = (wm_ref, wr_ref) if d == 0 else (dst, dst_r)
        return (
            remote(src, dst, f_send.at[d, part, 0], f_recv.at[d, part, 0], sib),
            remote(src_r, dst_r, f_send.at[d, part, 1], f_recv.at[d, part, 1], sib),
        )

    def far(back):
        out = []
        for n, d in enumerate((1, 3)):
            main, rest = spot(d if back is None else back, r)
            part = main.at[4 * n : 4 * n + 4]
            out.append(remote(part, part, h_send.at[n], h_recv.at[n], ring_peer(d)))
            if n == 0:
                out.append(remote(rest, rest, h_send.at[2], h_recv.at[2], ring_peer(d)))
        return out

    def far_copies():
        return far(None)

    def far_arrivals():
        return far(2)

    a_sib = remote(am_ref.at[1 - r], ab.at[x, z, r], sib_send, sib_recv, sib)
    a_sib.start()
    a_own = pltpu.make_async_copy(am_ref.at[r], ab.at[x, z, r], own_sem.at[0])
    a_own.start()
    for part in range(2):
        for d in (1, 3):
            for c in w_copies(d, part, 0):
                c.start()
    for c in forwards(0, r):
        c.start()
    own_w, own_wr = spot(0, r)
    w_own = pltpu.make_async_copy(wm_ref, own_w, own_sem.at[1])
    w_own.start()
    wr_own = pltpu.make_async_copy(wr_ref, own_wr, own_sem.at[2])
    wr_own.start()
    a_own.wait()
    remote(am_ref.at[r], ab.at[x, z, 1 - r], sib_send, sib_recv, sib).wait_recv()

    def x_peer(d):
        return (r, (lax.rem(x + d, 4) * 4 + z) * RING + y)

    def z_peer(d):
        return (r, (x * 4 + lax.rem(z + d, 4)) * RING + y)

    def a_peer(n, d):
        return x_peer(d) if n == 0 else z_peer(d)

    def a_first(n, d, back):
        sx, sz = lax.rem(x + 4 - back, 4), lax.rem(z + 4 - back, 4)
        part = ab.at[sx, z, 0] if n == 0 else ab.at[x, sz, 1]
        return remote(part, part, a_send.at[0, n, d], a_recv.at[0, n, d], a_peer(n, d))

    def a_second(n, d, back):
        sx, sz = lax.rem(x + 4 - back, 4), lax.rem(z + 4 - back, 4)
        part = ab.at[:, sz, 0] if n == 0 else ab.at[sx, :, 1]
        return remote(part, part, a_send.at[1, n, d], a_recv.at[1, n, d], a_peer(1 - n, d))

    def a_third(n, d, back):
        sx, sz = lax.rem(x + 4 - back, 4), lax.rem(z + 4 - back, 4)
        pick = slice(0, 2) if d == 1 else slice(2, 4)
        part = ab.at[pick, sz, 0] if n == 0 else ab.at[sx, pick, 1]
        return remote(part, part, a_send.at[2, n, d], a_recv.at[2, n, d], a_peer(1 - n, d))

    for d in (1, 3, 2):
        for n in range(2):
            a_first(n, d, 0).start()
    for n in range(2):
        for d in (1, 3, 2):
            a_first(n, d, d).wait_recv()
        for d in (1, 3):
            a_second(n, d, 0).start()

    def energies(h, c):
        for j in range(2 * RING):
            orbital_j = j_ref[q * 2 * RING + j]
            for i in range(HALF):
                orbital_i = i_ref[r * HALF + i]
                label = jnp.bitwise_xor(jnp.bitwise_xor(h, irrep_ref[orbital_i]), irrep_ref[orbital_j])
                energy = occ_ref[orbital_i] + occ_ref[orbital_j]
                dtab[h, i : i + 1, j * VH : (j + 1) * VH] = energy - table_ref[label]
        dtab[h, :, RING * COLS :] = jnp.ones((HALF, PAD), F32)
        dtab[h] = pltpu.roll(dtab[h], phase, 1)
        return c

    lax.fori_loop(0, IRREPS, energies, 0)
    for n in range(2):
        for d in (1, 3):
            a_second(n, d, d).wait_recv()
            a_third(n, d, d).start()
    for n in range(2):
        for d in (1, 3):
            a_third(n, d, 2).wait_recv()

    lane_group = lax.div(lax.broadcasted_iota(jnp.int32, (BLOCK, LANES), 1), 16)

    def build(g, c):
        for i in range(HALF):
            h = jnp.bitwise_xor(g, irrep_ref[i_ref[r * HALF + i]])
            hx, hz = lax.div(h, 2), 2 * lax.rem(h, 2)
            base = i * BLOCK
            for half in range(2):
                for lt in range(3):
                    lanes = slice(half * MAIN + lt * LANES, half * MAIN + (lt + 1) * LANES)
                    parts = [
                        ab[hx, hz + zp, half, lt * 25 + 3 * i : lt * 25 + 3 * i + 3].astype(F32).reshape(24, LANES)
                        for zp in range(2)
                    ] + [ab[hx, hz + zp, half, lt * 25 + 24].astype(F32) for zp in range(2)]
                    left[g, base : base + BLOCK, lanes] = jnp.concatenate(parts, axis=0).astype(BF16)
                tails = [ab[hx, hz + zp, half, 75:79].astype(F32).reshape(32, LANES) for zp in range(2)]
                parts = [t[0:24] for t in tails] + [jnp.broadcast_to(t[24:25], (8, LANES)) for t in tails]
                tail = jnp.concatenate(parts, axis=0)
                place = jnp.bitwise_xor(g, irrep_ref[k_ref[2 * half + 1]])
                tail = pltpu.roll(tail, lax.rem(16 * (place - i) + LANES, LANES), 1)
                tail = jnp.where(lane_group == place, tail, 0.0)
                lanes = slice(2 * MAIN + half * LANES, 2 * MAIN + (half + 1) * LANES)
                left[g, base : base + BLOCK, lanes] = tail.astype(BF16)
        return c

    lax.fori_loop(0, IRREPS, build, 0)
    w_own.wait()
    wr_own.wait()
    for c in forwards(0, 1 - r):
        c.wait_recv()

    lo, hi = 0, 0
    for value in range(RING):
        picked = is_value(y, value)
        lo = lo + picked * sum(ORDER[value][p] * 16**p for p in range(7))
        hi = hi + picked * sum(ORDER[value][p + 7] * 16**p for p in range(6))
    row_index = lax.broadcasted_iota(jnp.int32, (8, LANES), 0)
    NT = (((1,), (1,)), ((), ()))

    def out_copy(p, t, peer):
        return snd.at[p, peer], o_ref.at[q * TILES + t]

    def step(p, carry):
        lo, hi = carry
        t = lax.rem(lo, 16)

        def neighbours(part):
            for d in (1, 3):
                for c in w_copies(d, part, d):
                    c.wait_recv()
                for c in forwards(d, r, part):
                    c.start()
            if part == 1:
                for c in far_copies():
                    c.start()
            for d in (1, 3):
                for c in forwards(d, 1 - r, part):
                    c.wait_recv()

        @pl.when(p == 2)
        def _():
            neighbours(0)

        @pl.when(p == 6)
        def _():
            neighbours(1)

        @pl.when(p == 9)
        def _():
            for c in far_arrivals():
                c.wait_recv()
            for c in forwards(2, r):
                c.start()
            for c in forwards(2, 1 - r):
                c.wait_recv()

        window = pl.ds(pl.multiple_of(t * LANES + PAD - phase, 16), LANES)

        def multiply(g, c):
            total = lax.dot_general(
                left[g, :, 0 : 2 * MAIN], wb[g, window, :], NT, preferred_element_type=F32
            )
            total = total + lax.dot_general(
                left[g, :, 2 * MAIN :], wrb[window, :], NT, preferred_element_type=F32
            )
            acc[g] = total.reshape(HALF, BLOCK, LANES)
            return c

        lax.fori_loop(0, IRREPS, multiply, 0)
        lanes = pl.ds(pl.multiple_of(t * LANES, LANES), LANES)

        def finish(s, c):
            h = 2 * lax.rem(x + lax.div(s, 2), 4) + lax.rem(lax.div(z, 2) + s, 2)
            values = [acc[jnp.bitwise_xor(h, irrep_ref[i_ref[r * HALF + i]]), i] for i in range(HALF)]
            energy = dtab[h, :, lanes]
            for zp in range(2):
                first = ROWS * (8 * h + 4 * zp + y)
                last = jnp.zeros((8, LANES), F32)
                for i in range(HALF):
                    last = jnp.where(row_index == i, values[i][48 + 8 * zp : 56 + 8 * zp], last)
                snd[p, 2 * h + zp, 24] = (last / (energy - virt_ref[first + 24])).astype(BF16)
                for n in range(3):
                    top = 24 * zp + 8 * n
                    tiles = jnp.stack([v[top : top + 8] for v in values]).transpose(1, 0, 2)
                    for m in range(8):
                        value = tiles[m] / (energy - virt_ref[first + 8 * n + m])
                        snd[p, 2 * h + zp, 8 * n + m] = value.astype(BF16)
            return c

        lax.fori_loop(0, IRREPS, finish, 0)
        for ox, oz in SENDS:
            peer = lax.rem(x + ox, 4) * 4 + lax.rem(z + oz, 4)
            src, dst = out_copy(p, t, peer)
            remote(src, dst, o_send.at[peer], o_recv.at[q], (r, peer * RING + y)).start()
        src, dst = out_copy(p, t, q)
        pltpu.make_async_copy(src, dst, o_send.at[q]).start()
        return lax.div(lo, 16) + lax.rem(hi, 16) * 16**6, lax.div(hi, 16)

    lax.fori_loop(0, TILES, step, (lo, hi))

    a_sib.wait_send()
    for d in (0, 2):
        for c in forwards(d, r):
            c.wait_send()
    for d in (1, 3):
        for part in range(2):
            for c in (*forwards(d, r, part), *w_copies(d, part, 0)):
                c.wait_send()
    for c in far_copies():
        c.wait_send()
    for n in range(2):
        for d in (1, 3, 2):
            a_first(n, d, 0).wait_send()
        for d in (1, 3):
            a_second(n, d, 0).wait_send()
            a_third(n, d, d).wait_send()

    def all_tiles(peer):
        return o_ref.at[pl.ds(peer * TILES, TILES)]

    def drain_out(o, c):
        peer = plane_peer(o)
        whole = all_tiles(peer)
        remote(whole, whole, o_send.at[peer], o_recv.at[peer], sib).wait_send()
        remote(whole, whole, o_send.at[peer], o_recv.at[peer], sib).wait_recv()
        return c

    lax.fori_loop(1, PLANE, drain_out, 0)
    own = all_tiles(q)
    pltpu.make_async_copy(own, own, o_send.at[q]).wait()


def exchange(irrep, i, j, k, occ, virt, wm, wr, am):
    vm = pl.BlockSpec(memory_space=pltpu.VMEM)
    sm = pl.BlockSpec(memory_space=pltpu.SMEM)
    hbm = pl.BlockSpec(memory_space=pl.ANY)
    dma = pltpu.SemaphoreType.DMA
    return pl.pallas_call(
        main_kernel,
        out_shape=jax.ShapeDtypeStruct((PLANE * TILES, ROWS, 8, LANES), BF16),
        in_specs=[sm, sm, sm, sm, sm, sm, vm, hbm, hbm, hbm],
        out_specs=hbm,
        scratch_shapes=[
            pltpu.VMEM((IRREPS, RING * COLS + 2 * PAD, 2 * MAIN), BF16),
            pltpu.VMEM((RING * COLS + 2 * PAD, 2 * LANES), BF16),
            pltpu.VMEM((4, 4, 2, PIECES, 8, LANES), BF16),
            pltpu.VMEM((IRREPS, HALF * BLOCK, 2 * MAIN + 2 * LANES), BF16),
            pltpu.VMEM((IRREPS, HALF, BLOCK, LANES), F32),
            pltpu.VMEM((TILES, PLANE, ROWS, 8, LANES), BF16),
            pltpu.VMEM((IRREPS, HALF, WIN), F32),
            dma, dma, dma((3,)), dma((3, 2, 4)), dma((3, 2, 4)),
            dma((RING, 2, 2)), dma((RING, 2, 2)), dma((3,)), dma((3,)), dma((RING, 2, 2)), dma((RING, 2, 2)),
            dma((PLANE,)), dma((PLANE,)),
        ],
        compiler_params=pltpu.CompilerParams(
            collective_id=0, has_side_effects=True, vmem_limit_bytes=60 << 20
        ),
        name="exchange",
    )(irrep, i, j, k, occ, virt, virt.reshape(IRREPS, 1, VH), wm, wr, am)


def unpack_kernel(o_hbm, out_ref, o_ref, middle, sem, in_sem):
    low = lax.broadcasted_iota(jnp.int32, (ROWS, 8, LANES), 2) < PAD

    def place(src, tile, n):
        lanes = pl.ds(pl.multiple_of(tile * LANES, LANES), LANES)
        return pltpu.make_async_copy(src, out_ref.at[:, :, lanes], sem.at[n])

    def load(n):
        part = pl.ds(n * 2 * TILES, 2 * TILES)
        return pltpu.make_async_copy(o_hbm.at[part], o_ref.at[part], in_sem.at[n])

    for n in range(PLANE // 2):
        load(n).start()

    def pair(n, c):
        load(n).wait()
        for t in range(TILES - 1):
            place(o_ref.at[n * 2 * TILES + t], n * 25 + t, 0).start()
            place(o_ref.at[n * 2 * TILES + TILES + 1 + t], n * 25 + TILES + t, 0).start()
        even = o_ref[n * 2 * TILES + TILES - 1].astype(F32)
        odd = o_ref[n * 2 * TILES + TILES].astype(F32)
        middle[n] = jnp.where(low, even, odd).astype(BF16)
        place(middle.at[n], n * 25 + TILES - 1, 0).start()
        return c

    lax.fori_loop(0, PLANE // 2, pair, 0)
    pltpu.make_async_copy(out_ref, out_ref, sem.at[0]).wait()


def unpack(o):
    return pl.pallas_call(
        unpack_kernel,
        out_shape=jax.ShapeDtypeStruct((ROWS, HALF, RING * COLS * PLANE), BF16),
        in_specs=[pl.BlockSpec(memory_space=pl.ANY)],
        out_specs=pl.BlockSpec(memory_space=pl.ANY),
        scratch_shapes=[
            pltpu.VMEM((PLANE * TILES, ROWS, 8, LANES), BF16),
            pltpu.VMEM((PLANE // 2, ROWS, 8, LANES), BF16),
            pltpu.SemaphoreType.DMA((1,)),
            pltpu.SemaphoreType.DMA((PLANE // 2,)),
        ],
        compiler_params=pltpu.CompilerParams(vmem_limit_bytes=58 << 20),
        name="unpack",
    )(o)


def per_device(
    amplitudes, intermediate, occ_irrep, i_window, j_window, k_window, occ_energy, virt_energy
):
    wm, wr, am = pack(occ_irrep, k_window, intermediate.reshape(COLS, -1), amplitudes)
    o = exchange(
        occ_irrep, i_window, j_window, k_window, occ_energy, virt_energy, wm, wr, am
    )
    return unpack(o).transpose(1, 0, 2)


def solution(mesh):
    return jax.shard_map(
        per_device,
        mesh=mesh,
        in_specs=(P("rep", "tensor", None), P("tensor", None, "rep"), P(), P(), P(), P(), P(), P()),
        out_specs=P("rep", "tensor", None),
        check_vma=False,
    )
```

```python
import functools
import jax
import jax.numpy as jnp
from jax import lax
from jax.experimental import pallas as pl
from jax.experimental.pallas import tpu as pltpu
from jax.sharding import PartitionSpec as P

IRREPS = 8
VH = 200
ROWS = 25
HALF = 8
PLANE = 16
RING = 4
COLS = 400
LANES = 128
MAIN = 384
TILES = 13
HALVES = 13
WIN = TILES * LANES
PIECES = 79
PAD = 64
BLOCK = 64
MESH = pl.DeviceIdType.MESH
F32 = jnp.float32
BF16 = jnp.bfloat16
ORDER = (
    (1, 2, 3, 4, 11, 0, 5, 10, 12, 6, 7, 8, 9),
    (4, 5, 3, 2, 6, 7, 0, 1, 8, 9, 10, 11, 12),
    (7, 8, 6, 5, 9, 10, 4, 11, 12, 0, 1, 2, 3),
    (10, 11, 12, 9, 8, 0, 1, 7, 2, 3, 4, 5, 6),
)
PARTS = {1: ((144, 256), (0, 144)), 3: ((0, 256), (256, 144))}
THIRD = {1: (0, 3), 3: (1, 2)}
SENDS = (
    (2, 2), (2, 1), (1, 2), (2, 3), (3, 2), (1, 1), (3, 3), (1, 3),
    (3, 1), (2, 0), (0, 2), (1, 0), (0, 1), (3, 0), (0, 3),
)


def pack_kernel(
    irrep_ref, k_ref, w_ref, a_ref, wm_ref, wr_ref, am_ref, wm, wr, am, rows, last, rest, sem
):
    r = lax.axis_index("rep")
    for k in range(2):
        label = irrep_ref[k_ref[2 * r + k]]
        for h in range(IRREPS):
            first = (k * IRREPS + h) * VH
            g = jnp.bitwise_xor(label, h)
            if k == 0:
                wm[g, :, 0:VH] = w_ref[:, first : first + VH]
            else:
                wm[g, :, VH:MAIN] = w_ref[:, first : first + MAIN - VH]
                wr[:, h * 16 : (h + 1) * 16] = w_ref[:, first + MAIN - VH : first + VH]
    copies = [
        pltpu.make_async_copy(wm, wm_ref, sem.at[0]),
        pltpu.make_async_copy(wr, wr_ref, sem.at[1]),
        pltpu.make_async_copy(am, am_ref, sem.at[2]),
    ]
    copies[0].start()
    copies[1].start()
    for half in range(2):
        rest[...] = jnp.zeros_like(rest)
        for i in range(HALF):
            first = (half * HALF + i) * VH
            rows[0:ROWS, 0:VH] = a_ref[0, :, first : first + VH].astype(F32)
            rows[0:ROWS, VH:COLS] = a_ref[1, :, first : first + VH].astype(F32)
            for lt in range(3):
                lanes = slice(lt * LANES, (lt + 1) * LANES)
                am[half, lt * 25 + 3 * i : lt * 25 + 3 * i + 3] = (
                    rows[0:24, lanes].reshape(3, 8, LANES).astype(BF16)
                )
                last[lt, i : i + 1, :] = rows[24:25, lanes]
            rest[0:ROWS, i * 16 : (i + 1) * 16] = rows[0:ROWS, MAIN:COLS]
        for lt in range(3):
            am[half, lt * 25 + 24] = last[lt].astype(BF16)
        am[half, 75:79] = rest[...].reshape(4, 8, LANES).astype(BF16)
    copies[2].start()
    for c in copies:
        c.wait()


def pack(irrep, k, w, a):
    vm = pl.BlockSpec(memory_space=pltpu.VMEM)
    sm = pl.BlockSpec(memory_space=pltpu.SMEM)
    hbm = pl.BlockSpec(memory_space=pl.ANY)
    shapes = ((IRREPS, COLS, MAIN), (COLS, LANES), (2, PIECES, 8, LANES))
    return pl.pallas_call(
        pack_kernel,
        out_shape=tuple(jax.ShapeDtypeStruct(shape, BF16) for shape in shapes),
        in_specs=[sm, sm, vm, vm],
        out_specs=(hbm, hbm, hbm),
        scratch_shapes=[
            *(pltpu.VMEM(shape, BF16) for shape in shapes),
            pltpu.VMEM((32, 512), F32),
            pltpu.VMEM((3, 8, LANES), F32),
            pltpu.VMEM((32, LANES), F32),
            pltpu.SemaphoreType.DMA((3,)),
        ],
        compiler_params=pltpu.CompilerParams(vmem_limit_bytes=58 << 20),
        name="pack",
    )(irrep, k, w, a)


def is_value(y, value):
    return 1 - lax.div(lax.rem(y - value + RING, RING) + RING - 1, RING)


def main_kernel(
    irrep_ref, i_ref, j_ref, k_ref, occ_ref, virt_ref, line_ref, wm_ref, wr_ref, am_ref, o_ref,
    wb, wrb, ab, left, acc, snd, dtab, table_ref,
    sib_send, sib_recv, own_sem, a_send, a_recv,
    w_send, w_recv, h_send, h_recv, f_send, f_recv, o_send, o_recv, e_send, e_recv,
):
    r = lax.axis_index("rep")
    col = lax.axis_index("tensor")
    q = lax.div(col, RING)
    y = lax.rem(col, RING)
    x, z = lax.div(q, 4), lax.rem(q, 4)
    phase = PAD * lax.rem(q, 2)
    sib = (1 - r, col)

    def plane_peer(o):
        px, pz = lax.rem(x + lax.div(o, 4), 4), lax.rem(z + lax.rem(o, 4), 4)
        return px * 4 + pz

    def ring_peer(d):
        return (r, q * RING + lax.rem(y + d, RING))

    barrier = pltpu.get_barrier_semaphore()

    def greet(o, c):
        pl.semaphore_signal(barrier, inc=1, device_id=(r, plane_peer(o) * RING + y), device_id_type=MESH)
        return c

    lax.fori_loop(1, PLANE, greet, 0)
    for d in (1, 3):
        pl.semaphore_signal(barrier, inc=1, device_id=ring_peer(d), device_id_type=MESH)
    pl.semaphore_signal(barrier, inc=1, device_id=sib, device_id_type=MESH)
    pl.semaphore_wait(barrier, PLANE - 1 + 2 + 1)

    def remote(src, dst, ss, rs, dev):
        return pltpu.make_async_remote_copy(
            src_ref=src, dst_ref=dst, send_sem=ss, recv_sem=rs, device_id=dev, device_id_type=MESH
        )

    def spot(back, half, first=0, size=COLS):
        top = PAD + COLS * lax.rem(y + RING - back, RING) + first
        rows = pl.ds(pl.multiple_of(top, 16), size)
        lanes = pl.ds(pl.multiple_of(MAIN * half, LANES), MAIN)
        rest = pl.ds(pl.multiple_of(LANES * half, LANES), LANES)
        return wb.at[:, rows, lanes], wrb.at[rows, rest]

    def w_copies(d, part, back):
        first, size = PARTS[d][part]
        rows = pl.ds(first, size)
        dst, dst_r = spot(back, r, first, size)
        return (
            remote(wm_ref.at[:, rows], dst, w_send.at[d, part, 0], w_recv.at[d, part, 0], ring_peer(d)),
            remote(wr_ref.at[rows], dst_r, w_send.at[d, part, 1], w_recv.at[d, part, 1], ring_peer(d)),
        )

    def forwards(d, half, part=0):
        first, size = PARTS[d][part] if d in PARTS else (0, COLS)
        dst, dst_r = spot(d, half, first, size)
        src, src_r = (wm_ref, wr_ref) if d == 0 else (dst, dst_r)
        return (
            remote(src, dst, f_send.at[d, part, 0], f_recv.at[d, part, 0], sib),
            remote(src_r, dst_r, f_send.at[d, part, 1], f_recv.at[d, part, 1], sib),
        )

    def far(back):
        out = []
        for n, d in enumerate((1, 3)):
            main, rest = spot(d if back is None else back, r)
            part = main.at[4 * n : 4 * n + 4]
            out.append(remote(part, part, h_send.at[n], h_recv.at[n], ring_peer(d)))
            if n == 0:
                out.append(remote(rest, rest, h_send.at[2], h_recv.at[2], ring_peer(d)))
        return out

    def far_copies():
        return far(None)

    def far_arrivals():
        return far(2)

    a_sib = remote(am_ref.at[1 - r], ab.at[x, z, r], sib_send, sib_recv, sib)
    a_sib.start()
    a_own = pltpu.make_async_copy(am_ref.at[r], ab.at[x, z, r], own_sem.at[0])
    a_own.start()
    for part in range(2):
        for d in (1, 3):
            for c in w_copies(d, part, 0):
                c.start()
    for c in forwards(0, r):
        c.start()
    own_w, own_wr = spot(0, r)
    w_own = pltpu.make_async_copy(wm_ref, own_w, own_sem.at[1])
    w_own.start()
    wr_own = pltpu.make_async_copy(wr_ref, own_wr, own_sem.at[2])
    wr_own.start()
    a_own.wait()

    def x_peer(d):
        return (r, (lax.rem(x + d, 4) * 4 + z) * RING + y)

    def z_peer(d):
        return (r, (x * 4 + lax.rem(z + d, 4)) * RING + y)

    def a_peer(n, d):
        return x_peer(d) if n == 0 else z_peer(d)

    def a_first(n, d, back):
        sx, sz = lax.rem(x + 4 - back, 4), lax.rem(z + 4 - back, 4)
        part = ab.at[sx, z, 0] if n == 0 else ab.at[x, sz, 1]
        return remote(part, part, a_send.at[0, n, d], a_recv.at[0, n, d], a_peer(n, d))

    def a_entry(n, fixed, offset):
        sx, sz = lax.rem(x + 4 - (offset if n == 0 else fixed), 4), lax.rem(z + 4 - (fixed if n == 0 else offset), 4)
        return ab.at[sx, sz, n]

    def a_second(n, d, back, offset):
        part = a_entry(n, back, offset)
        return remote(part, part, a_send.at[1 + offset, n, d], a_recv.at[1 + offset, n, d], a_peer(1 - n, d))

    def a_third(n, d, back, offset):
        part = a_entry(n, back, offset)
        return remote(part, part, a_send.at[5 + offset, n, d], a_recv.at[5 + offset, n, d], a_peer(1 - n, d))

    def a_second_start(n, offset):
        for d in (1, 3):
            a_second(n, d, 0, offset).start()

    def a_half_start(n):
        for d in (1, 3, 2):
            a_first(n, d, 0).start()
        a_second_start(n, 0)

    for n in range(2):
        pl.when(r == n)(functools.partial(a_half_start, n))
    remote(am_ref.at[r], ab.at[x, z, 1 - r], sib_send, sib_recv, sib).wait_recv()
    for n in range(2):
        pl.when(r != n)(functools.partial(a_half_start, n))
    for d in (1, 3, 2):
        for n in range(2):
            a_first(n, d, d).wait_recv()
            a_second_start(n, d)

    def energies(h, c):
        for j in range(2 * RING):
            orbital_j = j_ref[q * 2 * RING + j]
            for i in range(HALF):
                orbital_i = i_ref[r * HALF + i]
                label = jnp.bitwise_xor(jnp.bitwise_xor(h, irrep_ref[orbital_i]), irrep_ref[orbital_j])
                energy = occ_ref[orbital_i] + occ_ref[orbital_j]
                dtab[h, i : i + 1, j * VH : (j + 1) * VH] = energy - table_ref[label]
        dtab[h, :, RING * COLS :] = jnp.ones((HALF, PAD), F32)
        dtab[h] = pltpu.roll(dtab[h], phase, 1)
        return c

    for h in range(IRREPS):
        table_ref[h] = line_ref[h * VH : (h + 1) * VH].reshape(1, VH)
    lax.fori_loop(0, IRREPS, energies, 0)
    for offset in (0, 1, 3, 2):
        for n in range(2):
            for d in (1, 3):
                a_second(n, d, d, offset).wait_recv()
                if offset in THIRD[d]:
                    a_third(n, d, d, offset).start()
    for d in (1, 3):
        for offset in THIRD[d]:
            for n in range(2):
                a_third(n, d, 2, offset).wait_recv()

    lane_group = lax.div(lax.broadcasted_iota(jnp.int32, (BLOCK, LANES), 1), 16)

    def build(g, c):
        for i in range(HALF):
            h = jnp.bitwise_xor(g, irrep_ref[i_ref[r * HALF + i]])
            hx, hz = lax.div(h, 2), 2 * lax.rem(h, 2)
            base = i * BLOCK
            for half in range(2):
                for lt in range(3):
                    lanes = slice(half * MAIN + lt * LANES, half * MAIN + (lt + 1) * LANES)
                    parts = [
                        ab[hx, hz + zp, half, lt * 25 + 3 * i : lt * 25 + 3 * i + 3].astype(F32).reshape(24, LANES)
                        for zp in range(2)
                    ] + [ab[hx, hz + zp, half, lt * 25 + 24].astype(F32) for zp in range(2)]
                    left[g, base : base + BLOCK, lanes] = jnp.concatenate(parts, axis=0).astype(BF16)
                tails = [ab[hx, hz + zp, half, 75:79].astype(F32).reshape(32, LANES) for zp in range(2)]
                parts = [t[0:24] for t in tails] + [jnp.broadcast_to(t[24:25], (8, LANES)) for t in tails]
                tail = jnp.concatenate(parts, axis=0)
                place = jnp.bitwise_xor(g, irrep_ref[k_ref[2 * half + 1]])
                tail = pltpu.roll(tail, lax.rem(16 * (place - i) + LANES, LANES), 1)
                tail = jnp.where(lane_group == place, tail, 0.0)
                lanes = slice(2 * MAIN + half * LANES, 2 * MAIN + (half + 1) * LANES)
                left[g, base : base + BLOCK, lanes] = tail.astype(BF16)
        return c

    lax.fori_loop(0, IRREPS, build, 0)
    w_own.wait()
    wr_own.wait()
    for c in forwards(0, 1 - r):
        c.wait_recv()

    lo, hi = 0, 0
    for value in range(RING):
        picked = is_value(y, value)
        lo = lo + picked * sum(ORDER[value][p] * 16**p for p in range(7))
        hi = hi + picked * sum(ORDER[value][p + 7] * 16**p for p in range(6))
    row_index = lax.broadcasted_iota(jnp.int32, (8, LANES), 0)
    NT = (((1,), (1,)), ((), ()))

    def out_copy(p, t, peer):
        return snd.at[p, peer], o_ref.at[q * TILES + t]

    def half_copy(p, t, peer):
        return snd.at[p, peer, 0:HALVES], o_ref.at[q * TILES + t, 0:HALVES]

    edge = (TILES - 1) * (1 - lax.rem(q, 2))
    lane = lax.broadcasted_iota(jnp.int32, (8, LANES), 1)
    kept = lax.div(lane, PAD) == lax.rem(q, 2)

    def step(p, carry):
        lo, hi = carry
        t = lax.rem(lo, 16)

        def neighbours(part):
            for d in (1, 3):
                for c in w_copies(d, part, d):
                    c.wait_recv()
                for c in forwards(d, r, part):
                    c.start()
            if part == 1:
                for c in far_copies():
                    c.start()
            for d in (1, 3):
                for c in forwards(d, 1 - r, part):
                    c.wait_recv()

        @pl.when(p == 2)
        def _():
            neighbours(0)

        @pl.when(p == 6)
        def _():
            neighbours(1)

        @pl.when(p == 9)
        def _():
            for c in far_arrivals():
                c.wait_recv()
            for c in forwards(2, r):
                c.start()
            for c in forwards(2, 1 - r):
                c.wait_recv()

        window = pl.ds(pl.multiple_of(t * LANES + PAD - phase, 16), LANES)

        def multiply(g, c):
            right = jnp.concatenate([wb[g, window, :], wrb[window, :]], axis=1)
            total = lax.dot_general(left[g], right, NT, preferred_element_type=F32)
            acc[g] = total.reshape(HALF, BLOCK, LANES)
            return c

        lax.fori_loop(0, IRREPS, multiply, 0)
        lanes = pl.ds(pl.multiple_of(t * LANES, LANES), LANES)

        def finish(s, c):
            h = 2 * lax.rem(x + lax.div(s, 2), 4) + lax.rem(lax.div(z, 2) + s, 2)
            values = [acc[jnp.bitwise_xor(h, irrep_ref[i_ref[r * HALF + i]]), i] for i in range(HALF)]
            energy = dtab[h, :, lanes]
            for zp in range(2):
                first = ROWS * (8 * h + 4 * zp + y)
                last = jnp.zeros((8, LANES), F32)
                for i in range(HALF):
                    last = jnp.where(row_index == i, values[i][48 + 8 * zp : 56 + 8 * zp], last)
                snd[p, 2 * h + zp, 24] = (last / (energy - virt_ref[first + 24])).astype(BF16)
                for n in range(3):
                    top = 24 * zp + 8 * n
                    tiles = jnp.stack([v[top : top + 8] for v in values]).transpose(1, 0, 2)
                    for m in range(8):
                        value = tiles[m] / (energy - virt_ref[first + 8 * n + m])
                        snd[p, 2 * h + zp, 8 * n + m] = value.astype(BF16)
            return c

        lax.fori_loop(0, IRREPS, finish, 0)
        @pl.when(t == edge)
        def _():
            def halve(peer, c):
                for m in range(HALVES - 1):
                    first = snd[p, peer, 2 * m].astype(F32)
                    second = pltpu.roll(snd[p, peer, 2 * m + 1].astype(F32), PAD, 1)
                    snd[p, peer, m] = jnp.where(kept, first, second).astype(BF16)
                snd[p, peer, HALVES - 1] = snd[p, peer, ROWS - 1]
                return c

            lax.fori_loop(0, PLANE, halve, 0)
            for ox, oz in SENDS:
                peer = lax.rem(x + ox, 4) * 4 + lax.rem(z + oz, 4)
                src, dst = half_copy(p, t, peer)
                remote(src, dst, e_send.at[peer], e_recv.at[q], (r, peer * RING + y)).start()
            src, dst = half_copy(p, t, q)
            pltpu.make_async_copy(src, dst, e_send.at[q]).start()

        @pl.when(t != edge)
        def _():
            for ox, oz in SENDS:
                peer = lax.rem(x + ox, 4) * 4 + lax.rem(z + oz, 4)
                src, dst = out_copy(p, t, peer)
                remote(src, dst, o_send.at[peer], o_recv.at[q], (r, peer * RING + y)).start()
            src, dst = out_copy(p, t, q)
            pltpu.make_async_copy(src, dst, o_send.at[q]).start()

        return lax.div(lo, 16) + lax.rem(hi, 16) * 16**6, lax.div(hi, 16)

    lax.fori_loop(0, TILES, step, (lo, hi))

    a_sib.wait_send()
    for d in (0, 2):
        for c in forwards(d, r):
            c.wait_send()
    for d in (1, 3):
        for part in range(2):
            for c in (*forwards(d, r, part), *w_copies(d, part, 0)):
                c.wait_send()
    for c in far_copies():
        c.wait_send()
    for n in range(2):
        for d in (1, 3, 2):
            a_first(n, d, 0).wait_send()
        for d in (1, 3):
            for offset in range(4):
                a_second(n, d, 0, offset).wait_send()
            for offset in THIRD[d]:
                a_third(n, d, d, offset).wait_send()

    def all_tiles(peer):
        first = peer * TILES + lax.rem(peer, 2)
        return o_ref.at[pl.ds(first, TILES - 1)]

    def edge_tile(peer):
        return o_ref.at[peer * TILES + (TILES - 1) * (1 - lax.rem(peer, 2)), 0:HALVES]

    def drain_out(o, c):
        peer = plane_peer(o)
        whole, part = all_tiles(peer), edge_tile(peer)
        for copy in (
            remote(whole, whole, o_send.at[peer], o_recv.at[peer], sib),
            remote(part, part, e_send.at[peer], e_recv.at[peer], sib),
        ):
            copy.wait_send()
            copy.wait_recv()
        return c

    lax.fori_loop(1, PLANE, drain_out, 0)
    own, part = all_tiles(q), edge_tile(q)
    pltpu.make_async_copy(own, own, o_send.at[q]).wait()
    pltpu.make_async_copy(part, part, e_send.at[q]).wait()


def exchange(irrep, i, j, k, occ, virt, wm, wr, am):
    vm = pl.BlockSpec(memory_space=pltpu.VMEM)
    sm = pl.BlockSpec(memory_space=pltpu.SMEM)
    hbm = pl.BlockSpec(memory_space=pl.ANY)
    dma = pltpu.SemaphoreType.DMA
    return pl.pallas_call(
        main_kernel,
        out_shape=jax.ShapeDtypeStruct((PLANE * TILES, ROWS, 8, LANES), BF16),
        in_specs=[sm, sm, sm, sm, sm, sm, vm, hbm, hbm, hbm],
        out_specs=hbm,
        scratch_shapes=[
            pltpu.VMEM((IRREPS, RING * COLS + 2 * PAD, 2 * MAIN), BF16),
            pltpu.VMEM((RING * COLS + 2 * PAD, 2 * LANES), BF16),
            pltpu.VMEM((4, 4, 2, PIECES, 8, LANES), BF16),
            pltpu.VMEM((IRREPS, HALF * BLOCK, 2 * MAIN + 2 * LANES), BF16),
            pltpu.VMEM((IRREPS, HALF, BLOCK, LANES), F32),
            pltpu.VMEM((TILES, PLANE, ROWS, 8, LANES), BF16),
            pltpu.VMEM((IRREPS, HALF, WIN), F32),
            pltpu.VMEM((IRREPS, 1, VH), F32),
            dma, dma, dma((3,)), dma((9, 2, 4)), dma((9, 2, 4)),
            dma((RING, 2, 2)), dma((RING, 2, 2)), dma((3,)), dma((3,)), dma((RING, 2, 2)), dma((RING, 2, 2)),
            dma((PLANE,)), dma((PLANE,)), dma((PLANE,)), dma((PLANE,)),
        ],
        compiler_params=pltpu.CompilerParams(
            collective_id=0, has_side_effects=True, vmem_limit_bytes=60 << 20
        ),
        name="exchange",
    )(irrep, i, j, k, occ, virt, virt, wm, wr, am)


def unpack_kernel(o_hbm, out_ref, o_ref, middle, sem, in_sem):
    low = lax.broadcasted_iota(jnp.int32, (8, LANES), 1) < PAD

    def place(src, tile, n):
        lanes = pl.ds(pl.multiple_of(tile * LANES, LANES), LANES)
        return pltpu.make_async_copy(src, out_ref.at[:, :, lanes], sem.at[n])

    def load(n):
        part = pl.ds(n * 2 * TILES, 2 * TILES)
        return pltpu.make_async_copy(o_hbm.at[part], o_ref.at[part], in_sem.at[n])

    for n in range(PLANE // 2):
        load(n).start()

    def pair(n, c):
        load(n).wait()
        for t in range(TILES - 1):
            place(o_ref.at[n * 2 * TILES + t], n * 25 + t, 0).start()
            place(o_ref.at[n * 2 * TILES + TILES + 1 + t], n * 25 + TILES + t, 0).start()
        for m in range(HALVES):
            even = o_ref[n * 2 * TILES + TILES - 1, m].astype(F32)
            odd = o_ref[n * 2 * TILES + TILES, m].astype(F32)
            middle[n, 2 * m] = jnp.where(low, even, odd).astype(BF16)
            if m < HALVES - 1:
                middle[n, 2 * m + 1] = pltpu.roll(jnp.where(low, odd, even), PAD, 1).astype(BF16)
        place(middle.at[n], n * 25 + TILES - 1, 0).start()
        return c

    lax.fori_loop(0, PLANE // 2, pair, 0)
    pltpu.make_async_copy(out_ref, out_ref, sem.at[0]).wait()


def unpack(o):
    return pl.pallas_call(
        unpack_kernel,
        out_shape=jax.ShapeDtypeStruct((ROWS, HALF, RING * COLS * PLANE), BF16),
        in_specs=[pl.BlockSpec(memory_space=pl.ANY)],
        out_specs=pl.BlockSpec(memory_space=pl.ANY),
        scratch_shapes=[
            pltpu.VMEM((PLANE * TILES, ROWS, 8, LANES), BF16),
            pltpu.VMEM((PLANE // 2, ROWS, 8, LANES), BF16),
            pltpu.SemaphoreType.DMA((1,)),
            pltpu.SemaphoreType.DMA((PLANE // 2,)),
        ],
        compiler_params=pltpu.CompilerParams(vmem_limit_bytes=58 << 20),
        name="unpack",
    )(o)


def per_device(
    amplitudes, intermediate, occ_irrep, i_window, j_window, k_window, occ_energy, virt_energy
):
    wm, wr, am = pack(occ_irrep, k_window, intermediate.reshape(COLS, -1), amplitudes)
    o = exchange(
        occ_irrep, i_window, j_window, k_window, occ_energy, virt_energy, wm, wr, am
    )
    return unpack(o).transpose(1, 0, 2)


def solution(mesh):
    return jax.shard_map(
        per_device,
        mesh=mesh,
        in_specs=(P("rep", "tensor", None), P("tensor", None, "rep"), P(), P(), P(), P(), P(), P()),
        out_specs=P("rep", "tensor", None),
        check_vma=False,
    )
```

```python
import functools
import jax
import jax.numpy as jnp
from jax import lax
from jax.experimental import pallas as pl
from jax.experimental.pallas import tpu as pltpu
from jax.sharding import PartitionSpec as P

IRREPS = 8
VH = 200
ROWS = 25
HALF = 8
PLANE = 16
RING = 4
COLS = 400
LANES = 128
MAIN = 384
TILES = 13
HALVES = 13
WIN = TILES * LANES
PIECES = 79
PAD = 64
BLOCK = 64
MESH = pl.DeviceIdType.MESH
F32 = jnp.float32
BF16 = jnp.bfloat16
ORDER = (
    (1, 2, 3, 4, 11, 0, 5, 10, 12, 6, 7, 8, 9),
    (4, 5, 3, 2, 6, 7, 0, 1, 8, 9, 10, 11, 12),
    (7, 8, 6, 5, 9, 10, 4, 11, 12, 0, 1, 2, 3),
    (10, 11, 12, 9, 8, 0, 1, 7, 2, 3, 4, 5, 6),
)
PARTS = {1: ((144, 256), (0, 144)), 3: ((0, 256), (256, 144))}
THIRD = {1: (0, 3), 3: (1, 2)}
SENDS = (
    (2, 2), (2, 1), (1, 2), (2, 3), (3, 2), (1, 1), (3, 3), (1, 3),
    (3, 1), (2, 0), (0, 2), (1, 0), (0, 1), (3, 0), (0, 3),
)


def pack_kernel(
    irrep_ref, k_ref, w_ref, a_ref, wm_ref, wr_ref, am_ref, wm, wr, am, wide, rows, last, rest, sem
):
    r = lax.axis_index("rep")
    for k in range(2):
        label = irrep_ref[k_ref[2 * r + k]]
        for h in range(IRREPS):
            first = (k * IRREPS + h) * VH
            g = jnp.bitwise_xor(label, h)
            if k == 0:
                wm[g, :, 0:VH] = w_ref[:, first : first + VH]
            else:
                wm[g, :, VH:MAIN] = w_ref[:, first : first + MAIN - VH]
                wr[:, h * 16 : (h + 1) * 16] = w_ref[:, first + MAIN - VH : first + VH]
    copies = [
        pltpu.make_async_copy(wm, wm_ref, sem.at[0]),
        pltpu.make_async_copy(wr, wr_ref, sem.at[1]),
        pltpu.make_async_copy(am, am_ref, sem.at[2]),
    ]
    copies[0].start()
    copies[1].start()
    for k in range(2):
        wide[k, 0:ROWS, :] = a_ref[:, k, :].astype(F32)
    for half in range(2):
        rest[...] = jnp.zeros_like(rest)
        for i in range(HALF):
            first = (half * HALF + i) * VH
            rows[0:ROWS, 0:VH] = wide[0, 0:ROWS, first : first + VH]
            rows[0:ROWS, VH:COLS] = wide[1, 0:ROWS, first : first + VH]
            for lt in range(3):
                lanes = slice(lt * LANES, (lt + 1) * LANES)
                am[half, lt * 25 + 3 * i : lt * 25 + 3 * i + 3] = (
                    rows[0:24, lanes].reshape(3, 8, LANES).astype(BF16)
                )
                last[lt, i : i + 1, :] = rows[24:25, lanes]
            rest[0:ROWS, i * 16 : (i + 1) * 16] = rows[0:ROWS, MAIN:COLS]
        for lt in range(3):
            am[half, lt * 25 + 24] = last[lt].astype(BF16)
        am[half, 75:79] = rest[...].reshape(4, 8, LANES).astype(BF16)
    copies[2].start()
    for c in copies:
        c.wait()


def pack(irrep, k, w, a):
    vm = pl.BlockSpec(memory_space=pltpu.VMEM)
    sm = pl.BlockSpec(memory_space=pltpu.SMEM)
    hbm = pl.BlockSpec(memory_space=pl.ANY)
    shapes = ((IRREPS, COLS, MAIN), (COLS, LANES), (2, PIECES, 8, LANES))
    return pl.pallas_call(
        pack_kernel,
        out_shape=tuple(jax.ShapeDtypeStruct(shape, BF16) for shape in shapes),
        in_specs=[sm, sm, vm, vm],
        out_specs=(hbm, hbm, hbm),
        scratch_shapes=[
            *(pltpu.VMEM(shape, BF16) for shape in shapes),
            pltpu.VMEM((2, 32, a.shape[2]), F32),
            pltpu.VMEM((32, 512), F32),
            pltpu.VMEM((3, 8, LANES), F32),
            pltpu.VMEM((32, LANES), F32),
            pltpu.SemaphoreType.DMA((3,)),
        ],
        compiler_params=pltpu.CompilerParams(vmem_limit_bytes=58 << 20),
        name="pack",
    )(irrep, k, w, a)


def is_value(y, value):
    return 1 - lax.div(lax.rem(y - value + RING, RING) + RING - 1, RING)


def main_kernel(
    irrep_ref, i_ref, j_ref, k_ref, occ_ref, virt_ref, line_ref, wm_ref, wr_ref, am_ref, o_ref,
    wb, wrb, ab, left, acc, snd, dtab, table_ref,
    sib_send, sib_recv, own_sem, a_send, a_recv,
    w_send, w_recv, h_send, h_recv, f_send, f_recv, o_send, o_recv, e_send, e_recv,
):
    r = lax.axis_index("rep")
    col = lax.axis_index("tensor")
    q = lax.div(col, RING)
    y = lax.rem(col, RING)
    x, z = lax.div(q, 4), lax.rem(q, 4)
    phase = PAD * lax.rem(q, 2)
    sib = (1 - r, col)

    def plane_peer(o):
        px, pz = lax.rem(x + lax.div(o, 4), 4), lax.rem(z + lax.rem(o, 4), 4)
        return px * 4 + pz

    def ring_peer(d):
        return (r, q * RING + lax.rem(y + d, RING))

    barrier = pltpu.get_barrier_semaphore()

    def greet(o, c):
        pl.semaphore_signal(barrier, inc=1, device_id=(r, plane_peer(o) * RING + y), device_id_type=MESH)
        return c

    lax.fori_loop(1, PLANE, greet, 0)
    for d in (1, 3):
        pl.semaphore_signal(barrier, inc=1, device_id=ring_peer(d), device_id_type=MESH)
    pl.semaphore_signal(barrier, inc=1, device_id=sib, device_id_type=MESH)
    pl.semaphore_wait(barrier, PLANE - 1 + 2 + 1)

    def remote(src, dst, ss, rs, dev):
        return pltpu.make_async_remote_copy(
            src_ref=src, dst_ref=dst, send_sem=ss, recv_sem=rs, device_id=dev, device_id_type=MESH
        )

    def spot(back, half, first=0, size=COLS):
        top = PAD + COLS * lax.rem(y + RING - back, RING) + first
        rows = pl.ds(pl.multiple_of(top, 16), size)
        lanes = pl.ds(pl.multiple_of(MAIN * half, LANES), MAIN)
        rest = pl.ds(pl.multiple_of(LANES * half, LANES), LANES)
        return wb.at[:, rows, lanes], wrb.at[rows, rest]

    def w_copies(d, part, back):
        first, size = PARTS[d][part]
        rows = pl.ds(first, size)
        dst, dst_r = spot(back, r, first, size)
        return (
            remote(wm_ref.at[:, rows], dst, w_send.at[d, part, 0], w_recv.at[d, part, 0], ring_peer(d)),
            remote(wr_ref.at[rows], dst_r, w_send.at[d, part, 1], w_recv.at[d, part, 1], ring_peer(d)),
        )

    def forwards(d, half, part=0):
        first, size = PARTS[d][part] if d in PARTS else (0, COLS)
        dst, dst_r = spot(d, half, first, size)
        src, src_r = (wm_ref, wr_ref) if d == 0 else (dst, dst_r)
        return (
            remote(src, dst, f_send.at[d, part, 0], f_recv.at[d, part, 0], sib),
            remote(src_r, dst_r, f_send.at[d, part, 1], f_recv.at[d, part, 1], sib),
        )

    def far(back):
        out = []
        for n, d in enumerate((1, 3)):
            main, rest = spot(d if back is None else back, r)
            part = main.at[4 * n : 4 * n + 4]
            out.append(remote(part, part, h_send.at[n], h_recv.at[n], ring_peer(d)))
            if n == 0:
                out.append(remote(rest, rest, h_send.at[2], h_recv.at[2], ring_peer(d)))
        return out

    def far_copies():
        return far(None)

    def far_arrivals():
        return far(2)

    a_sib = remote(am_ref.at[1 - r], ab.at[x, z, r], sib_send, sib_recv, sib)
    a_sib.start()
    a_own = pltpu.make_async_copy(am_ref.at[r], ab.at[x, z, r], own_sem.at[0])
    a_own.start()
    for part in range(2):
        for d in (1, 3):
            for c in w_copies(d, part, 0):
                c.start()
    for c in forwards(0, r):
        c.start()
    own_w, own_wr = spot(0, r)
    w_own = pltpu.make_async_copy(wm_ref, own_w, own_sem.at[1])
    w_own.start()
    wr_own = pltpu.make_async_copy(wr_ref, own_wr, own_sem.at[2])
    wr_own.start()
    a_own.wait()

    def x_peer(d):
        return (r, (lax.rem(x + d, 4) * 4 + z) * RING + y)

    def z_peer(d):
        return (r, (x * 4 + lax.rem(z + d, 4)) * RING + y)

    def a_peer(n, d):
        return x_peer(d) if n == 0 else z_peer(d)

    def a_first(n, d, back):
        sx, sz = lax.rem(x + 4 - back, 4), lax.rem(z + 4 - back, 4)
        part = ab.at[sx, z, 0] if n == 0 else ab.at[x, sz, 1]
        return remote(part, part, a_send.at[0, n, d], a_recv.at[0, n, d], a_peer(n, d))

    def a_entry(n, fixed, offset):
        sx, sz = lax.rem(x + 4 - (offset if n == 0 else fixed), 4), lax.rem(z + 4 - (fixed if n == 0 else offset), 4)
        return ab.at[sx, sz, n]

    def a_second(n, d, back, offset):
        part = a_entry(n, back, offset)
        return remote(part, part, a_send.at[1 + offset, n, d], a_recv.at[1 + offset, n, d], a_peer(1 - n, d))

    def a_third(n, d, back, offset):
        part = a_entry(n, back, offset)
        return remote(part, part, a_send.at[5 + offset, n, d], a_recv.at[5 + offset, n, d], a_peer(1 - n, d))

    def a_second_start(n, offset):
        for d in (1, 3):
            a_second(n, d, 0, offset).start()

    def a_half_start(n):
        for d in (1, 3, 2):
            a_first(n, d, 0).start()
        a_second_start(n, 0)

    for n in range(2):
        pl.when(r == n)(functools.partial(a_half_start, n))
    remote(am_ref.at[r], ab.at[x, z, 1 - r], sib_send, sib_recv, sib).wait_recv()
    for n in range(2):
        pl.when(r != n)(functools.partial(a_half_start, n))
    for d in (1, 3, 2):
        for n in range(2):
            a_first(n, d, d).wait_recv()
            a_second_start(n, d)

    def energies(h, c):
        for j in range(2 * RING):
            orbital_j = j_ref[q * 2 * RING + j]
            for i in range(HALF):
                orbital_i = i_ref[r * HALF + i]
                label = jnp.bitwise_xor(jnp.bitwise_xor(h, irrep_ref[orbital_i]), irrep_ref[orbital_j])
                energy = occ_ref[orbital_i] + occ_ref[orbital_j]
                dtab[h, i : i + 1, j * VH : (j + 1) * VH] = energy - table_ref[label]
        dtab[h, :, RING * COLS :] = jnp.ones((HALF, PAD), F32)
        dtab[h] = pltpu.roll(dtab[h], phase, 1)
        return c

    for h in range(IRREPS):
        table_ref[h] = line_ref[h * VH : (h + 1) * VH].reshape(1, VH)
    lax.fori_loop(0, IRREPS, energies, 0)
    for offset in (0, 1, 3, 2):
        for n in range(2):
            for d in (1, 3):
                a_second(n, d, d, offset).wait_recv()
                if offset in THIRD[d]:
                    a_third(n, d, d, offset).start()
    for d in (1, 3):
        for offset in THIRD[d]:
            for n in range(2):
                a_third(n, d, 2, offset).wait_recv()

    lane_group = lax.div(lax.broadcasted_iota(jnp.int32, (BLOCK, LANES), 1), 16)

    def build(g, c):
        for i in range(HALF):
            h = jnp.bitwise_xor(g, irrep_ref[i_ref[r * HALF + i]])
            hx, hz = lax.div(h, 2), 2 * lax.rem(h, 2)
            base = i * BLOCK
            for half in range(2):
                for lt in range(3):
                    lanes = slice(half * MAIN + lt * LANES, half * MAIN + (lt + 1) * LANES)
                    parts = [
                        ab[hx, hz + zp, half, lt * 25 + 3 * i : lt * 25 + 3 * i + 3].astype(F32).reshape(24, LANES)
                        for zp in range(2)
                    ] + [ab[hx, hz + zp, half, lt * 25 + 24].astype(F32) for zp in range(2)]
                    left[g, base : base + BLOCK, lanes] = jnp.concatenate(parts, axis=0).astype(BF16)
                tails = [ab[hx, hz + zp, half, 75:79].astype(F32).reshape(32, LANES) for zp in range(2)]
                parts = [t[0:24] for t in tails] + [jnp.broadcast_to(t[24:25], (8, LANES)) for t in tails]
                tail = jnp.concatenate(parts, axis=0)
                place = jnp.bitwise_xor(g, irrep_ref[k_ref[2 * half + 1]])
                tail = pltpu.roll(tail, lax.rem(16 * (place - i) + LANES, LANES), 1)
                tail = jnp.where(lane_group == place, tail, 0.0)
                lanes = slice(2 * MAIN + half * LANES, 2 * MAIN + (half + 1) * LANES)
                left[g, base : base + BLOCK, lanes] = tail.astype(BF16)
        return c

    lax.fori_loop(0, IRREPS, build, 0)
    w_own.wait()
    wr_own.wait()
    for c in forwards(0, 1 - r):
        c.wait_recv()

    lo, hi = 0, 0
    for value in range(RING):
        picked = is_value(y, value)
        lo = lo + picked * sum(ORDER[value][p] * 16**p for p in range(7))
        hi = hi + picked * sum(ORDER[value][p + 7] * 16**p for p in range(6))
    row_index = lax.broadcasted_iota(jnp.int32, (8, LANES), 0)
    NT = (((1,), (1,)), ((), ()))

    def out_copy(p, t, peer):
        return snd.at[p, peer], o_ref.at[q * TILES + t]

    def half_copy(p, t, peer):
        return snd.at[p, peer, 0:HALVES], o_ref.at[q * TILES + t, 0:HALVES]

    edge = (TILES - 1) * (1 - lax.rem(q, 2))
    lane = lax.broadcasted_iota(jnp.int32, (8, LANES), 1)
    kept = lax.div(lane, PAD) == lax.rem(q, 2)

    def step(p, carry):
        lo, hi = carry
        t = lax.rem(lo, 16)

        def neighbours(part):
            for d in (1, 3):
                for c in w_copies(d, part, d):
                    c.wait_recv()
                for c in forwards(d, r, part):
                    c.start()
            if part == 1:
                for c in far_copies():
                    c.start()
            for d in (1, 3):
                for c in forwards(d, 1 - r, part):
                    c.wait_recv()

        @pl.when(p == 2)
        def _():
            neighbours(0)

        @pl.when(p == 6)
        def _():
            neighbours(1)

        @pl.when(p == 9)
        def _():
            for c in far_arrivals():
                c.wait_recv()
            for c in forwards(2, r):
                c.start()
            for c in forwards(2, 1 - r):
                c.wait_recv()

        window = pl.ds(pl.multiple_of(t * LANES + PAD - phase, 16), LANES)

        def multiply(g, c):
            right = jnp.concatenate([wb[g, window, :], wrb[window, :]], axis=1)
            total = lax.dot_general(left[g], right, NT, preferred_element_type=F32)
            acc[g] = total.reshape(HALF, BLOCK, LANES)
            return c

        lax.fori_loop(0, IRREPS, multiply, 0)
        lanes = pl.ds(pl.multiple_of(t * LANES, LANES), LANES)

        def finish(s, c):
            h = 2 * lax.rem(x + lax.div(s, 2), 4) + lax.rem(lax.div(z, 2) + s, 2)
            values = [acc[jnp.bitwise_xor(h, irrep_ref[i_ref[r * HALF + i]]), i] for i in range(HALF)]
            energy = dtab[h, :, lanes]
            for zp in range(2):
                first = ROWS * (8 * h + 4 * zp + y)
                last = jnp.zeros((8, LANES), F32)
                for i in range(HALF):
                    last = jnp.where(row_index == i, values[i][48 + 8 * zp : 56 + 8 * zp], last)
                snd[p, 2 * h + zp, 24] = (last / (energy - virt_ref[first + 24])).astype(BF16)
                for n in range(3):
                    top = 24 * zp + 8 * n
                    tiles = jnp.stack([v[top : top + 8] for v in values]).transpose(1, 0, 2)
                    for m in range(8):
                        value = tiles[m] / (energy - virt_ref[first + 8 * n + m])
                        snd[p, 2 * h + zp, 8 * n + m] = value.astype(BF16)
            return c

        lax.fori_loop(0, IRREPS, finish, 0)
        @pl.when(t == edge)
        def _():
            def halve(peer, c):
                for m in range(HALVES - 1):
                    first = snd[p, peer, 2 * m].astype(F32)
                    second = pltpu.roll(snd[p, peer, 2 * m + 1].astype(F32), PAD, 1)
                    snd[p, peer, m] = jnp.where(kept, first, second).astype(BF16)
                snd[p, peer, HALVES - 1] = snd[p, peer, ROWS - 1]
                return c

            lax.fori_loop(0, PLANE, halve, 0)
            for ox, oz in SENDS:
                peer = lax.rem(x + ox, 4) * 4 + lax.rem(z + oz, 4)
                src, dst = half_copy(p, t, peer)
                remote(src, dst, e_send.at[peer], e_recv.at[q], (r, peer * RING + y)).start()
            src, dst = half_copy(p, t, q)
            pltpu.make_async_copy(src, dst, e_send.at[q]).start()

        @pl.when(t != edge)
        def _():
            for ox, oz in SENDS:
                peer = lax.rem(x + ox, 4) * 4 + lax.rem(z + oz, 4)
                src, dst = out_copy(p, t, peer)
                remote(src, dst, o_send.at[peer], o_recv.at[q], (r, peer * RING + y)).start()
            src, dst = out_copy(p, t, q)
            pltpu.make_async_copy(src, dst, o_send.at[q]).start()

        return lax.div(lo, 16) + lax.rem(hi, 16) * 16**6, lax.div(hi, 16)

    lax.fori_loop(0, TILES, step, (lo, hi))

    a_sib.wait_send()
    for d in (0, 2):
        for c in forwards(d, r):
            c.wait_send()
    for d in (1, 3):
        for part in range(2):
            for c in (*forwards(d, r, part), *w_copies(d, part, 0)):
                c.wait_send()
    for c in far_copies():
        c.wait_send()
    for n in range(2):
        for d in (1, 3, 2):
            a_first(n, d, 0).wait_send()
        for d in (1, 3):
            for offset in range(4):
                a_second(n, d, 0, offset).wait_send()
            for offset in THIRD[d]:
                a_third(n, d, d, offset).wait_send()

    def all_tiles(peer):
        first = peer * TILES + lax.rem(peer, 2)
        return o_ref.at[pl.ds(first, TILES - 1)]

    def edge_tile(peer):
        return o_ref.at[peer * TILES + (TILES - 1) * (1 - lax.rem(peer, 2)), 0:HALVES]

    def drain_out(o, c):
        peer = plane_peer(o)
        whole, part = all_tiles(peer), edge_tile(peer)
        for copy in (
            remote(whole, whole, o_send.at[peer], o_recv.at[peer], sib),
            remote(part, part, e_send.at[peer], e_recv.at[peer], sib),
        ):
            copy.wait_send()
            copy.wait_recv()
        return c

    lax.fori_loop(1, PLANE, drain_out, 0)
    own, part = all_tiles(q), edge_tile(q)
    pltpu.make_async_copy(own, own, o_send.at[q]).wait()
    pltpu.make_async_copy(part, part, e_send.at[q]).wait()


def exchange(irrep, i, j, k, occ, virt, wm, wr, am):
    vm = pl.BlockSpec(memory_space=pltpu.VMEM)
    sm = pl.BlockSpec(memory_space=pltpu.SMEM)
    hbm = pl.BlockSpec(memory_space=pl.ANY)
    dma = pltpu.SemaphoreType.DMA
    return pl.pallas_call(
        main_kernel,
        out_shape=jax.ShapeDtypeStruct((PLANE * TILES, ROWS, 8, LANES), BF16),
        in_specs=[sm, sm, sm, sm, sm, sm, vm, hbm, hbm, hbm],
        out_specs=hbm,
        scratch_shapes=[
            pltpu.VMEM((IRREPS, RING * COLS + 2 * PAD, 2 * MAIN), BF16),
            pltpu.VMEM((RING * COLS + 2 * PAD, 2 * LANES), BF16),
            pltpu.VMEM((4, 4, 2, PIECES, 8, LANES), BF16),
            pltpu.VMEM((IRREPS, HALF * BLOCK, 2 * MAIN + 2 * LANES), BF16),
            pltpu.VMEM((IRREPS, HALF, BLOCK, LANES), F32),
            pltpu.VMEM((TILES, PLANE, ROWS, 8, LANES), BF16),
            pltpu.VMEM((IRREPS, HALF, WIN), F32),
            pltpu.VMEM((IRREPS, 1, VH), F32),
            dma, dma, dma((3,)), dma((9, 2, 4)), dma((9, 2, 4)),
            dma((RING, 2, 2)), dma((RING, 2, 2)), dma((3,)), dma((3,)), dma((RING, 2, 2)), dma((RING, 2, 2)),
            dma((PLANE,)), dma((PLANE,)), dma((PLANE,)), dma((PLANE,)),
        ],
        compiler_params=pltpu.CompilerParams(
            collective_id=0, has_side_effects=True, vmem_limit_bytes=60 << 20
        ),
        name="exchange",
    )(irrep, i, j, k, occ, virt, virt, wm, wr, am)


def unpack_kernel(o_hbm, out_ref, o_ref, middle, sem, in_sem):
    low = lax.broadcasted_iota(jnp.int32, (8, LANES), 1) < PAD

    def place(src, tile, n):
        lanes = pl.ds(pl.multiple_of(tile * LANES, LANES), LANES)
        return pltpu.make_async_copy(src, out_ref.at[:, :, lanes], sem.at[n])

    def load(n):
        part = pl.ds(n * 2 * TILES, 2 * TILES)
        return pltpu.make_async_copy(o_hbm.at[part], o_ref.at[part], in_sem.at[n])

    for n in range(PLANE // 2):
        load(n).start()

    def pair(n, c):
        load(n).wait()
        for t in range(TILES - 1):
            place(o_ref.at[n * 2 * TILES + t], n * 25 + t, 0).start()
            place(o_ref.at[n * 2 * TILES + TILES + 1 + t], n * 25 + TILES + t, 0).start()
        for m in range(HALVES):
            even = o_ref[n * 2 * TILES + TILES - 1, m].astype(F32)
            odd = o_ref[n * 2 * TILES + TILES, m].astype(F32)
            middle[n, 2 * m] = jnp.where(low, even, odd).astype(BF16)
            if m < HALVES - 1:
                middle[n, 2 * m + 1] = pltpu.roll(jnp.where(low, odd, even), PAD, 1).astype(BF16)
        place(middle.at[n], n * 25 + TILES - 1, 0).start()
        return c

    lax.fori_loop(0, PLANE // 2, pair, 0)
    pltpu.make_async_copy(out_ref, out_ref, sem.at[0]).wait()


def unpack(o):
    return pl.pallas_call(
        unpack_kernel,
        out_shape=jax.ShapeDtypeStruct((ROWS, HALF, RING * COLS * PLANE), BF16),
        in_specs=[pl.BlockSpec(memory_space=pl.ANY)],
        out_specs=pl.BlockSpec(memory_space=pl.ANY),
        scratch_shapes=[
            pltpu.VMEM((PLANE * TILES, ROWS, 8, LANES), BF16),
            pltpu.VMEM((PLANE // 2, ROWS, 8, LANES), BF16),
            pltpu.SemaphoreType.DMA((1,)),
            pltpu.SemaphoreType.DMA((PLANE // 2,)),
        ],
        compiler_params=pltpu.CompilerParams(vmem_limit_bytes=58 << 20),
        name="unpack",
    )(o)


def per_device(
    amplitudes, intermediate, occ_irrep, i_window, j_window, k_window, occ_energy, virt_energy
):
    wm, wr, am = pack(occ_irrep, k_window, intermediate.reshape(COLS, -1), amplitudes.transpose(1, 0, 2))
    o = exchange(
        occ_irrep, i_window, j_window, k_window, occ_energy, virt_energy, wm, wr, am
    )
    return unpack(o).transpose(1, 0, 2)


def solution(mesh):
    return jax.shard_map(
        per_device,
        mesh=mesh,
        in_specs=(P("rep", "tensor", None), P("tensor", None, "rep"), P(), P(), P(), P(), P(), P()),
        out_specs=P("rep", "tensor", None),
        check_vma=False,
    )
```

```python
import functools
import jax
import jax.numpy as jnp
from jax import lax
from jax.experimental import pallas as pl
from jax.experimental.pallas import tpu as pltpu
from jax.sharding import PartitionSpec as P

IRREPS = 8
VH = 200
ROWS = 25
HALF = 8
PLANE = 16
RING = 4
COLS = 400
LANES = 128
MAIN = 384
TILES = 13
HALVES = 13
WIN = TILES * LANES
PIECES = 79
PAD = 64
BLOCK = 64
MESH = pl.DeviceIdType.MESH
F32 = jnp.float32
BF16 = jnp.bfloat16
ORDER = (
    (1, 2, 3, 4, 11, 0, 12, 5, 10, 6, 7, 8, 9),
    (4, 5, 3, 2, 6, 7, 1, 8, 0, 12, 9, 10, 11),
    (7, 8, 6, 5, 9, 10, 4, 11, 12, 0, 1, 2, 3),
    (10, 11, 9, 8, 1, 0, 12, 7, 2, 3, 4, 5, 6),
)
PARTS = {1: ((144, 256), (0, 144)), 3: ((0, 256), (256, 144))}
THIRD = {1: (0, 3), 3: (1, 2)}
SENDS = (
    (2, 2), (2, 1), (1, 2), (2, 3), (3, 2), (1, 1), (3, 3), (1, 3),
    (3, 1), (2, 0), (0, 2), (1, 0), (0, 1), (3, 0), (0, 3),
)


def pack_kernel(
    irrep_ref, k_ref, w_ref, a_ref, wm_ref, wr_ref, am_ref, wm, wr, am, wide, rows, last, rest, sem
):
    r = lax.axis_index("rep")
    for k in range(2):
        label = irrep_ref[k_ref[2 * r + k]]
        for h in range(IRREPS):
            first = (k * IRREPS + h) * VH
            g = jnp.bitwise_xor(label, h)
            if k == 0:
                wm[g, :, 0:VH] = w_ref[:, first : first + VH]
            else:
                wm[g, :, VH:MAIN] = w_ref[:, first : first + MAIN - VH]
                wr[:, h * 16 : (h + 1) * 16] = w_ref[:, first + MAIN - VH : first + VH]
    copies = [
        pltpu.make_async_copy(wm, wm_ref, sem.at[0]),
        pltpu.make_async_copy(wr, wr_ref, sem.at[1]),
        pltpu.make_async_copy(am, am_ref, sem.at[2]),
    ]
    copies[0].start()
    copies[1].start()
    for k in range(2):
        wide[k, 0:ROWS, :] = a_ref[:, k, :].astype(F32)
    for half in range(2):
        rest[...] = jnp.zeros_like(rest)
        for i in range(HALF):
            first = (half * HALF + i) * VH
            rows[0:ROWS, 0:VH] = wide[0, 0:ROWS, first : first + VH]
            rows[0:ROWS, VH:COLS] = wide[1, 0:ROWS, first : first + VH]
            for lt in range(3):
                lanes = slice(lt * LANES, (lt + 1) * LANES)
                am[half, lt * 25 + 3 * i : lt * 25 + 3 * i + 3] = (
                    rows[0:24, lanes].reshape(3, 8, LANES).astype(BF16)
                )
                last[lt, i : i + 1, :] = rows[24:25, lanes]
            rest[0:ROWS, i * 16 : (i + 1) * 16] = rows[0:ROWS, MAIN:COLS]
        for lt in range(3):
            am[half, lt * 25 + 24] = last[lt].astype(BF16)
        am[half, 75:79] = rest[...].reshape(4, 8, LANES).astype(BF16)
    copies[2].start()
    for c in copies:
        c.wait()


def pack(irrep, k, w, a):
    vm = pl.BlockSpec(memory_space=pltpu.VMEM)
    sm = pl.BlockSpec(memory_space=pltpu.SMEM)
    hbm = pl.BlockSpec(memory_space=pl.ANY)
    shapes = ((IRREPS, COLS, MAIN), (COLS, LANES), (2, PIECES, 8, LANES))
    return pl.pallas_call(
        pack_kernel,
        out_shape=tuple(jax.ShapeDtypeStruct(shape, BF16) for shape in shapes),
        in_specs=[sm, sm, vm, vm],
        out_specs=(hbm, hbm, hbm),
        scratch_shapes=[
            *(pltpu.VMEM(shape, BF16) for shape in shapes),
            pltpu.VMEM((2, 32, a.shape[2]), F32),
            pltpu.VMEM((32, 512), F32),
            pltpu.VMEM((3, 8, LANES), F32),
            pltpu.VMEM((32, LANES), F32),
            pltpu.SemaphoreType.DMA((3,)),
        ],
        compiler_params=pltpu.CompilerParams(vmem_limit_bytes=58 << 20),
        name="pack",
    )(irrep, k, w, a)


def is_value(y, value):
    return 1 - lax.div(lax.rem(y - value + RING, RING) + RING - 1, RING)


def main_kernel(
    irrep_ref, i_ref, j_ref, k_ref, occ_ref, virt_ref, line_ref, wm_ref, wr_ref, am_ref, o_ref,
    wb, wrb, ab, left, acc, snd, dtab, table_ref,
    sib_send, sib_recv, own_sem, a_send, a_recv,
    w_send, w_recv, h_send, h_recv, f_send, f_recv, o_send, o_recv, e_send, e_recv,
):
    r = lax.axis_index("rep")
    col = lax.axis_index("tensor")
    q = lax.div(col, RING)
    y = lax.rem(col, RING)
    x, z = lax.div(q, 4), lax.rem(q, 4)
    phase = PAD * lax.rem(q, 2)
    sib = (1 - r, col)

    def plane_peer(o):
        px, pz = lax.rem(x + lax.div(o, 4), 4), lax.rem(z + lax.rem(o, 4), 4)
        return px * 4 + pz

    def ring_peer(d):
        return (r, q * RING + lax.rem(y + d, RING))

    barrier = pltpu.get_barrier_semaphore()

    def greet(o, c):
        pl.semaphore_signal(barrier, inc=1, device_id=(r, plane_peer(o) * RING + y), device_id_type=MESH)
        return c

    lax.fori_loop(1, PLANE, greet, 0)
    for d in (1, 3):
        pl.semaphore_signal(barrier, inc=1, device_id=ring_peer(d), device_id_type=MESH)
    pl.semaphore_signal(barrier, inc=1, device_id=sib, device_id_type=MESH)
    pl.semaphore_wait(barrier, PLANE - 1 + 2 + 1)

    def remote(src, dst, ss, rs, dev):
        return pltpu.make_async_remote_copy(
            src_ref=src, dst_ref=dst, send_sem=ss, recv_sem=rs, device_id=dev, device_id_type=MESH
        )

    def spot(back, half, first=0, size=COLS):
        top = PAD + COLS * lax.rem(y + RING - back, RING) + first
        rows = pl.ds(pl.multiple_of(top, 16), size)
        lanes = pl.ds(pl.multiple_of(MAIN * half, LANES), MAIN)
        rest = pl.ds(pl.multiple_of(LANES * half, LANES), LANES)
        return wb.at[:, rows, lanes], wrb.at[rows, rest]

    def w_copies(d, part, back):
        first, size = PARTS[d][part]
        rows = pl.ds(first, size)
        dst, dst_r = spot(back, r, first, size)
        return (
            remote(wm_ref.at[:, rows], dst, w_send.at[d, part, 0], w_recv.at[d, part, 0], ring_peer(d)),
            remote(wr_ref.at[rows], dst_r, w_send.at[d, part, 1], w_recv.at[d, part, 1], ring_peer(d)),
        )

    def forwards(d, half, part=0):
        first, size = PARTS[d][part] if d in PARTS else (0, COLS)
        dst, dst_r = spot(d, half, first, size)
        src, src_r = (wm_ref, wr_ref) if d == 0 else (dst, dst_r)
        return (
            remote(src, dst, f_send.at[d, part, 0], f_recv.at[d, part, 0], sib),
            remote(src_r, dst_r, f_send.at[d, part, 1], f_recv.at[d, part, 1], sib),
        )

    def far(back):
        out = []
        for n, d in enumerate((1, 3)):
            main, rest = spot(d if back is None else back, r)
            part = main.at[4 * n : 4 * n + 4]
            out.append(remote(part, part, h_send.at[n], h_recv.at[n], ring_peer(d)))
            if n == 0:
                out.append(remote(rest, rest, h_send.at[2], h_recv.at[2], ring_peer(d)))
        return out

    def far_copies():
        return far(None)

    def far_arrivals():
        return far(2)

    a_sib = remote(am_ref.at[1 - r], ab.at[x, z, r], sib_send, sib_recv, sib)
    a_sib.start()
    a_own = pltpu.make_async_copy(am_ref.at[r], ab.at[x, z, r], own_sem.at[0])
    a_own.start()
    for part in range(2):
        for d in (1, 3):
            for c in w_copies(d, part, 0):
                c.start()
    for c in forwards(0, r):
        c.start()
    own_w, own_wr = spot(0, r)
    w_own = pltpu.make_async_copy(wm_ref, own_w, own_sem.at[1])
    w_own.start()
    wr_own = pltpu.make_async_copy(wr_ref, own_wr, own_sem.at[2])
    wr_own.start()
    a_own.wait()

    def x_peer(d):
        return (r, (lax.rem(x + d, 4) * 4 + z) * RING + y)

    def z_peer(d):
        return (r, (x * 4 + lax.rem(z + d, 4)) * RING + y)

    def a_peer(n, d):
        return x_peer(d) if n == 0 else z_peer(d)

    def a_first(n, d, back):
        sx, sz = lax.rem(x + 4 - back, 4), lax.rem(z + 4 - back, 4)
        part = ab.at[sx, z, 0] if n == 0 else ab.at[x, sz, 1]
        return remote(part, part, a_send.at[0, n, d], a_recv.at[0, n, d], a_peer(n, d))

    def a_entry(n, fixed, offset):
        sx, sz = lax.rem(x + 4 - (offset if n == 0 else fixed), 4), lax.rem(z + 4 - (fixed if n == 0 else offset), 4)
        return ab.at[sx, sz, n]

    def a_second(n, d, back, offset):
        part = a_entry(n, back, offset)
        return remote(part, part, a_send.at[1 + offset, n, d], a_recv.at[1 + offset, n, d], a_peer(1 - n, d))

    def a_third(n, d, back, offset):
        part = a_entry(n, back, offset)
        return remote(part, part, a_send.at[5 + offset, n, d], a_recv.at[5 + offset, n, d], a_peer(1 - n, d))

    def a_second_start(n, offset):
        for d in (1, 3):
            a_second(n, d, 0, offset).start()

    def a_half_start(n):
        for d in (1, 3, 2):
            a_first(n, d, 0).start()
        a_second_start(n, 0)

    for n in range(2):
        pl.when(r == n)(functools.partial(a_half_start, n))
    remote(am_ref.at[r], ab.at[x, z, 1 - r], sib_send, sib_recv, sib).wait_recv()
    for n in range(2):
        pl.when(r != n)(functools.partial(a_half_start, n))
    for d in (1, 3, 2):
        for n in range(2):
            a_first(n, d, d).wait_recv()
            a_second_start(n, d)

    def energies(h, c):
        for j in range(2 * RING):
            orbital_j = j_ref[q * 2 * RING + j]
            for i in range(HALF):
                orbital_i = i_ref[r * HALF + i]
                label = jnp.bitwise_xor(jnp.bitwise_xor(h, irrep_ref[orbital_i]), irrep_ref[orbital_j])
                energy = occ_ref[orbital_i] + occ_ref[orbital_j]
                dtab[h, i : i + 1, j * VH : (j + 1) * VH] = energy - table_ref[label]
        dtab[h, :, RING * COLS :] = jnp.ones((HALF, PAD), F32)
        dtab[h] = pltpu.roll(dtab[h], phase, 1)
        return c

    for h in range(IRREPS):
        table_ref[h] = line_ref[h * VH : (h + 1) * VH].reshape(1, VH)
    lax.fori_loop(0, IRREPS, energies, 0)
    for offset in (0, 1, 3, 2):
        for n in range(2):
            for d in (1, 3):
                a_second(n, d, d, offset).wait_recv()
                if offset in THIRD[d]:
                    a_third(n, d, d, offset).start()
    for d in (1, 3):
        for offset in THIRD[d]:
            for n in range(2):
                a_third(n, d, 2, offset).wait_recv()

    lane_group = lax.div(lax.broadcasted_iota(jnp.int32, (BLOCK, LANES), 1), 16)

    def build(g, c):
        for i in range(HALF):
            h = jnp.bitwise_xor(g, irrep_ref[i_ref[r * HALF + i]])
            hx, hz = lax.div(h, 2), 2 * lax.rem(h, 2)
            base = i * BLOCK
            for half in range(2):
                for lt in range(3):
                    lanes = slice(half * MAIN + lt * LANES, half * MAIN + (lt + 1) * LANES)
                    parts = [
                        ab[hx, hz + zp, half, lt * 25 + 3 * i : lt * 25 + 3 * i + 3].astype(F32).reshape(24, LANES)
                        for zp in range(2)
                    ] + [ab[hx, hz + zp, half, lt * 25 + 24].astype(F32) for zp in range(2)]
                    left[g, base : base + BLOCK, lanes] = jnp.concatenate(parts, axis=0).astype(BF16)
                tails = [ab[hx, hz + zp, half, 75:79].astype(F32).reshape(32, LANES) for zp in range(2)]
                parts = [t[0:24] for t in tails] + [jnp.broadcast_to(t[24:25], (8, LANES)) for t in tails]
                tail = jnp.concatenate(parts, axis=0)
                place = jnp.bitwise_xor(g, irrep_ref[k_ref[2 * half + 1]])
                tail = pltpu.roll(tail, lax.rem(16 * (place - i) + LANES, LANES), 1)
                tail = jnp.where(lane_group == place, tail, 0.0)
                lanes = slice(2 * MAIN + half * LANES, 2 * MAIN + (half + 1) * LANES)
                left[g, base : base + BLOCK, lanes] = tail.astype(BF16)
        return c

    lax.fori_loop(0, IRREPS, build, 0)
    w_own.wait()
    wr_own.wait()
    for c in forwards(0, 1 - r):
        c.wait_recv()

    lo, hi = 0, 0
    for value in range(RING):
        picked = is_value(y, value)
        lo = lo + picked * sum(ORDER[value][p] * 16**p for p in range(7))
        hi = hi + picked * sum(ORDER[value][p + 7] * 16**p for p in range(6))
    row_index = lax.broadcasted_iota(jnp.int32, (8, LANES), 0)
    NT = (((1,), (1,)), ((), ()))

    def out_copy(p, t, peer):
        return snd.at[p, peer], o_ref.at[q * TILES + t]

    def half_copy(p, t, peer):
        return snd.at[p, peer, 0:HALVES], o_ref.at[q * TILES + t, 0:HALVES]

    edge = (TILES - 1) * (1 - lax.rem(q, 2))
    lane = lax.broadcasted_iota(jnp.int32, (8, LANES), 1)
    kept = lax.div(lane, PAD) == lax.rem(q, 2)

    def step(p, carry):
        lo, hi = carry
        t = lax.rem(lo, 16)

        def neighbours(part):
            for d in (1, 3):
                for c in w_copies(d, part, d):
                    c.wait_recv()
                for c in forwards(d, r, part):
                    c.start()
            if part == 1:
                for c in far_copies():
                    c.start()
            for d in (1, 3):
                for c in forwards(d, 1 - r, part):
                    c.wait_recv()

        @pl.when(p == 2)
        def _():
            neighbours(0)

        @pl.when(p == 6)
        def _():
            neighbours(1)

        @pl.when(p == 9)
        def _():
            for c in far_arrivals():
                c.wait_recv()
            for c in forwards(2, r):
                c.start()
            for c in forwards(2, 1 - r):
                c.wait_recv()

        window = pl.ds(pl.multiple_of(t * LANES + PAD - phase, 16), LANES)

        def multiply(g, c):
            right = jnp.concatenate([wb[g, window, :], wrb[window, :]], axis=1)
            total = lax.dot_general(left[g], right, NT, preferred_element_type=F32)
            acc[g] = total.reshape(HALF, BLOCK, LANES)
            return c

        lax.fori_loop(0, IRREPS, multiply, 0)
        lanes = pl.ds(pl.multiple_of(t * LANES, LANES), LANES)

        def finish(s, c):
            h = 2 * lax.rem(x + lax.div(s, 2), 4) + lax.rem(lax.div(z, 2) + s, 2)
            values = [acc[jnp.bitwise_xor(h, irrep_ref[i_ref[r * HALF + i]]), i] for i in range(HALF)]
            energy = dtab[h, :, lanes]
            for zp in range(2):
                first = ROWS * (8 * h + 4 * zp + y)
                last = jnp.zeros((8, LANES), F32)
                for i in range(HALF):
                    last = jnp.where(row_index == i, values[i][48 + 8 * zp : 56 + 8 * zp], last)
                snd[p, 2 * h + zp, 24] = (last / (energy - virt_ref[first + 24])).astype(BF16)
                for n in range(3):
                    top = 24 * zp + 8 * n
                    tiles = jnp.stack([v[top : top + 8] for v in values]).transpose(1, 0, 2)
                    for m in range(8):
                        value = tiles[m] / (energy - virt_ref[first + 8 * n + m])
                        snd[p, 2 * h + zp, 8 * n + m] = value.astype(BF16)
            return c

        lax.fori_loop(0, IRREPS, finish, 0)
        @pl.when(t == edge)
        def _():
            def halve(peer, c):
                for m in range(HALVES - 1):
                    first = snd[p, peer, 2 * m].astype(F32)
                    second = pltpu.roll(snd[p, peer, 2 * m + 1].astype(F32), PAD, 1)
                    snd[p, peer, m] = jnp.where(kept, first, second).astype(BF16)
                snd[p, peer, HALVES - 1] = snd[p, peer, ROWS - 1]
                return c

            lax.fori_loop(0, PLANE, halve, 0)
            for ox, oz in SENDS:
                peer = lax.rem(x + ox, 4) * 4 + lax.rem(z + oz, 4)
                src, dst = half_copy(p, t, peer)
                remote(src, dst, e_send.at[peer], e_recv.at[q], (r, peer * RING + y)).start()
            src, dst = half_copy(p, t, q)
            pltpu.make_async_copy(src, dst, e_send.at[q]).start()

        @pl.when(t != edge)
        def _():
            for ox, oz in SENDS:
                peer = lax.rem(x + ox, 4) * 4 + lax.rem(z + oz, 4)
                src, dst = out_copy(p, t, peer)
                remote(src, dst, o_send.at[peer], o_recv.at[q], (r, peer * RING + y)).start()
            src, dst = out_copy(p, t, q)
            pltpu.make_async_copy(src, dst, o_send.at[q]).start()

        return lax.div(lo, 16) + lax.rem(hi, 16) * 16**6, lax.div(hi, 16)

    lax.fori_loop(0, TILES, step, (lo, hi))

    a_sib.wait_send()
    for d in (0, 2):
        for c in forwards(d, r):
            c.wait_send()
    for d in (1, 3):
        for part in range(2):
            for c in (*forwards(d, r, part), *w_copies(d, part, 0)):
                c.wait_send()
    for c in far_copies():
        c.wait_send()
    for n in range(2):
        for d in (1, 3, 2):
            a_first(n, d, 0).wait_send()
        for d in (1, 3):
            for offset in range(4):
                a_second(n, d, 0, offset).wait_send()
            for offset in THIRD[d]:
                a_third(n, d, d, offset).wait_send()

    def all_tiles(peer):
        first = peer * TILES + lax.rem(peer, 2)
        return o_ref.at[pl.ds(first, TILES - 1)]

    def edge_tile(peer):
        return o_ref.at[peer * TILES + (TILES - 1) * (1 - lax.rem(peer, 2)), 0:HALVES]

    def drain_out(o, c):
        peer = plane_peer(o)
        whole, part = all_tiles(peer), edge_tile(peer)
        for copy in (
            remote(whole, whole, o_send.at[peer], o_recv.at[peer], sib),
            remote(part, part, e_send.at[peer], e_recv.at[peer], sib),
        ):
            copy.wait_send()
            copy.wait_recv()
        return c

    lax.fori_loop(1, PLANE, drain_out, 0)
    own, part = all_tiles(q), edge_tile(q)
    pltpu.make_async_copy(own, own, o_send.at[q]).wait()
    pltpu.make_async_copy(part, part, e_send.at[q]).wait()


def exchange(irrep, i, j, k, occ, virt, wm, wr, am):
    vm = pl.BlockSpec(memory_space=pltpu.VMEM)
    sm = pl.BlockSpec(memory_space=pltpu.SMEM)
    hbm = pl.BlockSpec(memory_space=pl.ANY)
    dma = pltpu.SemaphoreType.DMA
    return pl.pallas_call(
        main_kernel,
        out_shape=jax.ShapeDtypeStruct((PLANE * TILES, ROWS, 8, LANES), BF16),
        in_specs=[sm, sm, sm, sm, sm, sm, vm, hbm, hbm, hbm],
        out_specs=hbm,
        scratch_shapes=[
            pltpu.VMEM((IRREPS, RING * COLS + 2 * PAD, 2 * MAIN), BF16),
            pltpu.VMEM((RING * COLS + 2 * PAD, 2 * LANES), BF16),
            pltpu.VMEM((4, 4, 2, PIECES, 8, LANES), BF16),
            pltpu.VMEM((IRREPS, HALF * BLOCK, 2 * MAIN + 2 * LANES), BF16),
            pltpu.VMEM((IRREPS, HALF, BLOCK, LANES), F32),
            pltpu.VMEM((TILES, PLANE, ROWS, 8, LANES), BF16),
            pltpu.VMEM((IRREPS, HALF, WIN), F32),
            pltpu.VMEM((IRREPS, 1, VH), F32),
            dma, dma, dma((3,)), dma((9, 2, 4)), dma((9, 2, 4)),
            dma((RING, 2, 2)), dma((RING, 2, 2)), dma((3,)), dma((3,)), dma((RING, 2, 2)), dma((RING, 2, 2)),
            dma((PLANE,)), dma((PLANE,)), dma((PLANE,)), dma((PLANE,)),
        ],
        compiler_params=pltpu.CompilerParams(
            collective_id=0, has_side_effects=True, vmem_limit_bytes=60 << 20
        ),
        name="exchange",
    )(irrep, i, j, k, occ, virt, virt, wm, wr, am)


def unpack_kernel(o_hbm, out_ref, o_ref, middle, sem, in_sem):
    low = lax.broadcasted_iota(jnp.int32, (8, LANES), 1) < PAD

    def place(src, tile, n):
        lanes = pl.ds(pl.multiple_of(tile * LANES, LANES), LANES)
        return pltpu.make_async_copy(src, out_ref.at[:, :, lanes], sem.at[n])

    def load(n):
        part = pl.ds(n * 2 * TILES, 2 * TILES)
        return pltpu.make_async_copy(o_hbm.at[part], o_ref.at[part], in_sem.at[n])

    for n in range(PLANE // 2):
        load(n).start()

    def pair(n, c):
        load(n).wait()
        for t in range(TILES - 1):
            place(o_ref.at[n * 2 * TILES + t], n * 25 + t, 0).start()
            place(o_ref.at[n * 2 * TILES + TILES + 1 + t], n * 25 + TILES + t, 0).start()
        for m in range(HALVES):
            even = o_ref[n * 2 * TILES + TILES - 1, m].astype(F32)
            odd = o_ref[n * 2 * TILES + TILES, m].astype(F32)
            middle[n, 2 * m] = jnp.where(low, even, odd).astype(BF16)
            if m < HALVES - 1:
                middle[n, 2 * m + 1] = pltpu.roll(jnp.where(low, odd, even), PAD, 1).astype(BF16)
        place(middle.at[n], n * 25 + TILES - 1, 0).start()
        return c

    lax.fori_loop(0, PLANE // 2, pair, 0)
    pltpu.make_async_copy(out_ref, out_ref, sem.at[0]).wait()


def unpack(o):
    return pl.pallas_call(
        unpack_kernel,
        out_shape=jax.ShapeDtypeStruct((ROWS, HALF, RING * COLS * PLANE), BF16),
        in_specs=[pl.BlockSpec(memory_space=pl.ANY)],
        out_specs=pl.BlockSpec(memory_space=pl.ANY),
        scratch_shapes=[
            pltpu.VMEM((PLANE * TILES, ROWS, 8, LANES), BF16),
            pltpu.VMEM((PLANE // 2, ROWS, 8, LANES), BF16),
            pltpu.SemaphoreType.DMA((1,)),
            pltpu.SemaphoreType.DMA((PLANE // 2,)),
        ],
        compiler_params=pltpu.CompilerParams(vmem_limit_bytes=58 << 20),
        name="unpack",
    )(o)


def per_device(
    amplitudes, intermediate, occ_irrep, i_window, j_window, k_window, occ_energy, virt_energy
):
    wm, wr, am = pack(occ_irrep, k_window, intermediate.reshape(COLS, -1), amplitudes.transpose(1, 0, 2))
    o = exchange(
        occ_irrep, i_window, j_window, k_window, occ_energy, virt_energy, wm, wr, am
    )
    return unpack(o).transpose(1, 0, 2)


def solution(mesh):
    return jax.shard_map(
        per_device,
        mesh=mesh,
        in_specs=(P("rep", "tensor", None), P("tensor", None, "rep"), P(), P(), P(), P(), P(), P()),
        out_specs=P("rep", "tensor", None),
        check_vma=False,
    )
```

```python
import functools
import jax
import jax.numpy as jnp
from jax import lax
from jax.experimental import pallas as pl
from jax.experimental.pallas import tpu as pltpu
from jax.sharding import PartitionSpec as P

IRREPS = 8
VH = 200
ROWS = 25
HALF = 8
PLANE = 16
RING = 4
COLS = 400
LANES = 128
MAIN = 384
TILES = 13
HALVES = 13
WIN = TILES * LANES
PIECES = 79
PAD = 64
BLOCK = 64
MESH = pl.DeviceIdType.MESH
F32 = jnp.float32
BF16 = jnp.bfloat16
ORDER = (
    (1, 2, 3, 4, 11, 0, 12, 5, 10, 6, 7, 8, 9),
    (4, 5, 3, 2, 6, 7, 1, 8, 0, 12, 9, 10, 11),
    (7, 8, 6, 5, 9, 10, 4, 11, 12, 0, 1, 2, 3),
    (10, 11, 9, 8, 1, 0, 12, 7, 2, 3, 4, 5, 6),
)
PARTS = {1: ((144, 256), (0, 144)), 3: ((0, 256), (256, 144))}
THIRD = {1: (0, 3), 3: (1, 2)}
SENDS = (
    (2, 2), (2, 1), (1, 2), (2, 3), (3, 2), (1, 1), (3, 3), (1, 3),
    (3, 1), (2, 0), (0, 2), (1, 0), (0, 1), (3, 0), (0, 3),
)


def pack_kernel(
    irrep_ref, k_ref, w_ref, a_ref, wm_ref, wr_ref, am_ref, wm, wr, am, wide, rows, last, rest, sem
):
    r = lax.axis_index("rep")
    for k in range(2):
        label = irrep_ref[k_ref[2 * r + k]]
        for h in range(IRREPS):
            first = (k * IRREPS + h) * VH
            g = jnp.bitwise_xor(label, h)
            if k == 0:
                wm[g, :, 0:VH] = w_ref[:, first : first + VH]
            else:
                wm[g, :, VH:MAIN] = w_ref[:, first : first + MAIN - VH]
                wr[:, h * 16 : (h + 1) * 16] = w_ref[:, first + MAIN - VH : first + VH]
    copies = [
        pltpu.make_async_copy(wm, wm_ref, sem.at[0]),
        pltpu.make_async_copy(wr, wr_ref, sem.at[1]),
        pltpu.make_async_copy(am, am_ref, sem.at[2]),
    ]
    copies[0].start()
    copies[1].start()
    for k in range(2):
        wide[k, 0:ROWS, :] = a_ref[:, k, :].astype(F32)
    for half in range(2):
        rest[...] = jnp.zeros_like(rest)
        for i in range(HALF):
            first = (half * HALF + i) * VH
            rows[0:ROWS, 0:VH] = wide[0, 0:ROWS, first : first + VH]
            rows[0:ROWS, VH:COLS] = wide[1, 0:ROWS, first : first + VH]
            for lt in range(3):
                lanes = slice(lt * LANES, (lt + 1) * LANES)
                am[half, lt * 25 + 3 * i : lt * 25 + 3 * i + 3] = (
                    rows[0:24, lanes].reshape(3, 8, LANES).astype(BF16)
                )
                last[lt, i : i + 1, :] = rows[24:25, lanes]
            rest[0:ROWS, i * 16 : (i + 1) * 16] = rows[0:ROWS, MAIN:COLS]
        for lt in range(3):
            am[half, lt * 25 + 24] = last[lt].astype(BF16)
        am[half, 75:79] = rest[...].reshape(4, 8, LANES).astype(BF16)
    copies[2].start()
    for c in copies:
        c.wait()


def pack(irrep, k, w, a):
    vm = pl.BlockSpec(memory_space=pltpu.VMEM)
    sm = pl.BlockSpec(memory_space=pltpu.SMEM)
    hbm = pl.BlockSpec(memory_space=pl.ANY)
    shapes = ((IRREPS, COLS, MAIN), (COLS, LANES), (2, PIECES, 8, LANES))
    return pl.pallas_call(
        pack_kernel,
        out_shape=tuple(jax.ShapeDtypeStruct(shape, BF16) for shape in shapes),
        in_specs=[sm, sm, vm, vm],
        out_specs=(hbm, hbm, hbm),
        scratch_shapes=[
            *(pltpu.VMEM(shape, BF16) for shape in shapes),
            pltpu.VMEM((2, 32, a.shape[2]), F32),
            pltpu.VMEM((32, 512), F32),
            pltpu.VMEM((3, 8, LANES), F32),
            pltpu.VMEM((32, LANES), F32),
            pltpu.SemaphoreType.DMA((3,)),
        ],
        compiler_params=pltpu.CompilerParams(vmem_limit_bytes=58 << 20),
        name="pack",
    )(irrep, k, w, a)


def is_value(y, value):
    return 1 - lax.div(lax.rem(y - value + RING, RING) + RING - 1, RING)


def main_kernel(
    irrep_ref, i_ref, j_ref, k_ref, occ_ref, virt_ref, line_ref, wm_ref, wr_ref, am_ref, o_ref,
    wb, wrb, ab, left, acc, snd, dtab, table_ref,
    sib_send, sib_recv, own_sem, a_send, a_recv,
    w_send, w_recv, h_send, h_recv, f_send, f_recv, o_send, o_recv, e_send, e_recv,
):
    r = lax.axis_index("rep")
    col = lax.axis_index("tensor")
    q = lax.div(col, RING)
    y = lax.rem(col, RING)
    x, z = lax.div(q, 4), lax.rem(q, 4)
    phase = PAD * lax.rem(q, 2)
    sib = (1 - r, col)

    def plane_peer(o):
        px, pz = lax.rem(x + lax.div(o, 4), 4), lax.rem(z + lax.rem(o, 4), 4)
        return px * 4 + pz

    def ring_peer(d):
        return (r, q * RING + lax.rem(y + d, RING))

    barrier = pltpu.get_barrier_semaphore()

    def greet(o, c):
        pl.semaphore_signal(barrier, inc=1, device_id=(r, plane_peer(o) * RING + y), device_id_type=MESH)
        return c

    lax.fori_loop(1, PLANE, greet, 0)
    for d in (1, 3):
        pl.semaphore_signal(barrier, inc=1, device_id=ring_peer(d), device_id_type=MESH)
    pl.semaphore_signal(barrier, inc=1, device_id=sib, device_id_type=MESH)
    pl.semaphore_wait(barrier, PLANE - 1 + 2 + 1)

    def remote(src, dst, ss, rs, dev):
        return pltpu.make_async_remote_copy(
            src_ref=src, dst_ref=dst, send_sem=ss, recv_sem=rs, device_id=dev, device_id_type=MESH
        )

    def spot(back, half, first=0, size=COLS):
        top = PAD + COLS * lax.rem(y + RING - back, RING) + first
        rows = pl.ds(pl.multiple_of(top, 16), size)
        lanes = pl.ds(pl.multiple_of(MAIN * half, LANES), MAIN)
        rest = pl.ds(pl.multiple_of(LANES * half, LANES), LANES)
        return wb.at[:, rows, lanes], wrb.at[rows, rest]

    def w_copies(d, part, back):
        first, size = PARTS[d][part]
        rows = pl.ds(first, size)
        dst, dst_r = spot(back, r, first, size)
        return (
            remote(wm_ref.at[:, rows], dst, w_send.at[d, part, 0], w_recv.at[d, part, 0], ring_peer(d)),
            remote(wr_ref.at[rows], dst_r, w_send.at[d, part, 1], w_recv.at[d, part, 1], ring_peer(d)),
        )

    def forwards(d, half, part=0):
        first, size = PARTS[d][part] if d in PARTS else (0, COLS)
        dst, dst_r = spot(d, half, first, size)
        src, src_r = (wm_ref, wr_ref) if d == 0 else (dst, dst_r)
        return (
            remote(src, dst, f_send.at[d, part, 0], f_recv.at[d, part, 0], sib),
            remote(src_r, dst_r, f_send.at[d, part, 1], f_recv.at[d, part, 1], sib),
        )

    def far(back):
        out = []
        for n, d in enumerate((1, 3)):
            main, rest = spot(d if back is None else back, r)
            part = main.at[4 * n : 4 * n + 4]
            out.append(remote(part, part, h_send.at[n], h_recv.at[n], ring_peer(d)))
            if n == 0:
                out.append(remote(rest, rest, h_send.at[2], h_recv.at[2], ring_peer(d)))
        return out

    def far_copies():
        return far(None)

    def far_arrivals():
        return far(2)

    a_sib = remote(am_ref.at[1 - r], ab.at[x, z, r], sib_send, sib_recv, sib)
    a_sib.start()
    a_own = pltpu.make_async_copy(am_ref.at[r], ab.at[x, z, r], own_sem.at[0])
    a_own.start()
    for part in range(2):
        for d in (1, 3):
            for c in w_copies(d, part, 0):
                c.start()
    for c in forwards(0, r):
        c.start()
    own_w, own_wr = spot(0, r)
    w_own = pltpu.make_async_copy(wm_ref, own_w, own_sem.at[1])
    w_own.start()
    wr_own = pltpu.make_async_copy(wr_ref, own_wr, own_sem.at[2])
    wr_own.start()
    a_own.wait()

    def x_peer(d):
        return (r, (lax.rem(x + d, 4) * 4 + z) * RING + y)

    def z_peer(d):
        return (r, (x * 4 + lax.rem(z + d, 4)) * RING + y)

    def a_peer(n, d):
        return x_peer(d) if n == 0 else z_peer(d)

    def a_first(n, d, back):
        sx, sz = lax.rem(x + 4 - back, 4), lax.rem(z + 4 - back, 4)
        part = ab.at[sx, z, 0] if n == 0 else ab.at[x, sz, 1]
        return remote(part, part, a_send.at[0, n, d], a_recv.at[0, n, d], a_peer(n, d))

    def a_entry(n, fixed, offset):
        sx, sz = lax.rem(x + 4 - (offset if n == 0 else fixed), 4), lax.rem(z + 4 - (fixed if n == 0 else offset), 4)
        return ab.at[sx, sz, n]

    def a_second(n, d, back, offset):
        part = a_entry(n, back, offset)
        return remote(part, part, a_send.at[1 + offset, n, d], a_recv.at[1 + offset, n, d], a_peer(1 - n, d))

    def a_third(n, d, back, offset):
        part = a_entry(n, back, offset)
        return remote(part, part, a_send.at[5 + offset, n, d], a_recv.at[5 + offset, n, d], a_peer(1 - n, d))

    def a_second_start(n, offset):
        for d in (1, 3):
            a_second(n, d, 0, offset).start()

    def a_half_start(n):
        for d in (1, 3, 2):
            a_first(n, d, 0).start()
        a_second_start(n, 0)

    for n in range(2):
        pl.when(r == n)(functools.partial(a_half_start, n))
    remote(am_ref.at[r], ab.at[x, z, 1 - r], sib_send, sib_recv, sib).wait_recv()
    for n in range(2):
        pl.when(r != n)(functools.partial(a_half_start, n))
    for d in (1, 3, 2):
        for n in range(2):
            a_first(n, d, d).wait_recv()
            a_second_start(n, d)

    def energies(h, c):
        for j in range(2 * RING):
            orbital_j = j_ref[q * 2 * RING + j]
            for i in range(HALF):
                orbital_i = i_ref[r * HALF + i]
                label = jnp.bitwise_xor(jnp.bitwise_xor(h, irrep_ref[orbital_i]), irrep_ref[orbital_j])
                energy = occ_ref[orbital_i] + occ_ref[orbital_j]
                dtab[h, i : i + 1, j * VH : (j + 1) * VH] = energy - table_ref[label]
        dtab[h, :, RING * COLS :] = jnp.ones((HALF, PAD), F32)
        dtab[h] = pltpu.roll(dtab[h], phase, 1)
        return c

    for h in range(IRREPS):
        table_ref[h] = line_ref[h * VH : (h + 1) * VH].reshape(1, VH)
    lax.fori_loop(0, IRREPS, energies, 0)
    for offset in (0, 1, 3, 2):
        for n in range(2):
            for d in (1, 3):
                a_second(n, d, d, offset).wait_recv()
                if offset in THIRD[d]:
                    a_third(n, d, d, offset).start()
    for d in (1, 3):
        for offset in THIRD[d]:
            for n in range(2):
                a_third(n, d, 2, offset).wait_recv()

    lane_group = lax.div(lax.broadcasted_iota(jnp.int32, (BLOCK, LANES), 1), 16)

    def build(g, c):
        for i in range(HALF):
            h = jnp.bitwise_xor(g, irrep_ref[i_ref[r * HALF + i]])
            hx, hz = lax.div(h, 2), 2 * lax.rem(h, 2)
            base = i * BLOCK
            for half in range(2):
                for lt in range(3):
                    lanes = slice(half * MAIN + lt * LANES, half * MAIN + (lt + 1) * LANES)
                    parts = [
                        ab[hx, hz + zp, half, lt * 25 + 3 * i : lt * 25 + 3 * i + 3].astype(F32).reshape(24, LANES)
                        for zp in range(2)
                    ] + [ab[hx, hz + zp, half, lt * 25 + 24].astype(F32) for zp in range(2)]
                    left[g, base : base + BLOCK, lanes] = jnp.concatenate(parts, axis=0).astype(BF16)
                tails = [ab[hx, hz + zp, half, 75:79].astype(F32).reshape(32, LANES) for zp in range(2)]
                parts = [t[0:24] for t in tails] + [jnp.broadcast_to(t[24:25], (8, LANES)) for t in tails]
                tail = jnp.concatenate(parts, axis=0)
                place = jnp.bitwise_xor(g, irrep_ref[k_ref[2 * half + 1]])
                tail = pltpu.roll(tail, lax.rem(16 * (place - i) + LANES, LANES), 1)
                tail = jnp.where(lane_group == place, tail, 0.0)
                lanes = slice(2 * MAIN + half * LANES, 2 * MAIN + (half + 1) * LANES)
                left[g, base : base + BLOCK, lanes] = tail.astype(BF16)
        return c

    lax.fori_loop(0, IRREPS, build, 0)
    w_own.wait()
    wr_own.wait()
    for c in forwards(0, 1 - r):
        c.wait_recv()

    lo, hi = 0, 0
    for value in range(RING):
        picked = is_value(y, value)
        lo = lo + picked * sum(ORDER[value][p] * 16**p for p in range(7))
        hi = hi + picked * sum(ORDER[value][p + 7] * 16**p for p in range(6))
    row_index = lax.broadcasted_iota(jnp.int32, (8, LANES), 0)
    NT = (((1,), (1,)), ((), ()))

    def out_copy(p, t, peer):
        return snd.at[p, peer], o_ref.at[q * TILES + t]

    def half_copy(p, t, peer):
        return snd.at[p, peer, 0:HALVES], o_ref.at[q * TILES + t, 0:HALVES]

    edge = (TILES - 1) * (1 - lax.rem(q, 2))
    lane = lax.broadcasted_iota(jnp.int32, (8, LANES), 1)
    kept = lax.div(lane, PAD) == lax.rem(q, 2)

    def step(p, carry):
        lo, hi = carry
        t = lax.rem(lo, 16)

        def neighbours(part):
            for d in (1, 3):
                for c in w_copies(d, part, d):
                    c.wait_recv()
                for c in forwards(d, r, part):
                    c.start()
            if part == 1:
                for c in far_copies():
                    c.start()
            for d in (1, 3):
                for c in forwards(d, 1 - r, part):
                    c.wait_recv()

        @pl.when(p == 2)
        def _():
            neighbours(0)

        @pl.when(p == 6)
        def _():
            neighbours(1)

        @pl.when(p == 9)
        def _():
            for c in far_arrivals():
                c.wait_recv()
            for c in forwards(2, r):
                c.start()
            for c in forwards(2, 1 - r):
                c.wait_recv()

        window = pl.ds(pl.multiple_of(t * LANES + PAD - phase, 16), LANES)

        def multiply(g, c):
            right = jnp.concatenate([wb[g, window, :], wrb[window, :]], axis=1)
            total = lax.dot_general(left[g], right, NT, preferred_element_type=F32)
            acc[g] = total.reshape(HALF, BLOCK, LANES)
            return c

        lax.fori_loop(0, IRREPS, multiply, 0)
        lanes = pl.ds(pl.multiple_of(t * LANES, LANES), LANES)

        def finish(s, c):
            h = 2 * lax.rem(x + lax.div(s, 2), 4) + lax.rem(lax.div(z, 2) + s, 2)
            values = [acc[jnp.bitwise_xor(h, irrep_ref[i_ref[r * HALF + i]]), i] for i in range(HALF)]
            energy = dtab[h, :, lanes]
            for zp in range(2):
                first = ROWS * (8 * h + 4 * zp + y)
                last = jnp.zeros((8, LANES), F32)
                for i in range(HALF):
                    last = jnp.where(row_index == i, values[i][48 + 8 * zp : 56 + 8 * zp], last)
                snd[p, 2 * h + zp, 24] = (last / (energy - virt_ref[first + 24])).astype(BF16)
                for n in range(3):
                    top = 24 * zp + 8 * n
                    tiles = jnp.stack([v[top : top + 8] for v in values]).transpose(1, 0, 2)
                    for m in range(8):
                        value = tiles[m] / (energy - virt_ref[first + 8 * n + m])
                        snd[p, 2 * h + zp, 8 * n + m] = value.astype(BF16)
            return c

        lax.fori_loop(0, IRREPS, finish, 0)
        @pl.when(t == edge)
        def _():
            def halve(peer, c):
                for m in range(HALVES - 1):
                    first = snd[p, peer, 2 * m].astype(F32)
                    second = pltpu.roll(snd[p, peer, 2 * m + 1].astype(F32), PAD, 1)
                    snd[p, peer, m] = jnp.where(kept, first, second).astype(BF16)
                snd[p, peer, HALVES - 1] = snd[p, peer, ROWS - 1]
                return c

            lax.fori_loop(0, PLANE, halve, 0)
            for ox, oz in SENDS:
                peer = lax.rem(x + ox, 4) * 4 + lax.rem(z + oz, 4)
                src, dst = half_copy(p, t, peer)
                remote(src, dst, e_send.at[peer], e_recv.at[q], (r, peer * RING + y)).start()
            src, dst = half_copy(p, t, q)
            pltpu.make_async_copy(src, dst, e_send.at[q]).start()

        @pl.when(t != edge)
        def _():
            for ox, oz in SENDS:
                peer = lax.rem(x + ox, 4) * 4 + lax.rem(z + oz, 4)
                src, dst = out_copy(p, t, peer)
                remote(src, dst, o_send.at[peer], o_recv.at[q], (r, peer * RING + y)).start()
            src, dst = out_copy(p, t, q)
            pltpu.make_async_copy(src, dst, o_send.at[q]).start()

        return lax.div(lo, 16) + lax.rem(hi, 16) * 16**6, lax.div(hi, 16)

    lax.fori_loop(0, TILES, step, (lo, hi))

    a_sib.wait_send()
    for d in (0, 2):
        for c in forwards(d, r):
            c.wait_send()
    for d in (1, 3):
        for part in range(2):
            for c in (*forwards(d, r, part), *w_copies(d, part, 0)):
                c.wait_send()
    for c in far_copies():
        c.wait_send()
    for n in range(2):
        for d in (1, 3, 2):
            a_first(n, d, 0).wait_send()
        for d in (1, 3):
            for offset in range(4):
                a_second(n, d, 0, offset).wait_send()
            for offset in THIRD[d]:
                a_third(n, d, d, offset).wait_send()

    def all_tiles(peer):
        first = peer * TILES + lax.rem(peer, 2)
        return o_ref.at[pl.ds(first, TILES - 1)]

    def edge_tile(peer):
        return o_ref.at[peer * TILES + (TILES - 1) * (1 - lax.rem(peer, 2)), 0:HALVES]

    def drain_out(o, c):
        peer = plane_peer(o)
        whole, part = all_tiles(peer), edge_tile(peer)
        for copy in (
            remote(whole, whole, o_send.at[peer], o_recv.at[peer], sib),
            remote(part, part, e_send.at[peer], e_recv.at[peer], sib),
        ):
            copy.wait_send()
            copy.wait_recv()
        return c

    lax.fori_loop(1, PLANE, drain_out, 0)
    own, part = all_tiles(q), edge_tile(q)
    pltpu.make_async_copy(own, own, o_send.at[q]).wait()
    pltpu.make_async_copy(part, part, e_send.at[q]).wait()


def exchange(irrep, i, j, k, occ, virt, wm, wr, am):
    vm = pl.BlockSpec(memory_space=pltpu.VMEM)
    sm = pl.BlockSpec(memory_space=pltpu.SMEM)
    hbm = pl.BlockSpec(memory_space=pl.ANY)
    dma = pltpu.SemaphoreType.DMA
    return pl.pallas_call(
        main_kernel,
        out_shape=jax.ShapeDtypeStruct((PLANE * TILES, ROWS, 8, LANES), BF16),
        in_specs=[sm, sm, sm, sm, sm, sm, vm, hbm, hbm, hbm],
        out_specs=hbm,
        scratch_shapes=[
            pltpu.VMEM((IRREPS, RING * COLS + 2 * PAD, 2 * MAIN), BF16),
            pltpu.VMEM((RING * COLS + 2 * PAD, 2 * LANES), BF16),
            pltpu.VMEM((4, 4, 2, PIECES, 8, LANES), BF16),
            pltpu.VMEM((IRREPS, HALF * BLOCK, 2 * MAIN + 2 * LANES), BF16),
            pltpu.VMEM((IRREPS, HALF, BLOCK, LANES), F32),
            pltpu.VMEM((TILES, PLANE, ROWS, 8, LANES), BF16),
            pltpu.VMEM((IRREPS, HALF, WIN), F32),
            pltpu.VMEM((IRREPS, 1, VH), F32),
            dma, dma, dma((3,)), dma((9, 2, 4)), dma((9, 2, 4)),
            dma((RING, 2, 2)), dma((RING, 2, 2)), dma((3,)), dma((3,)), dma((RING, 2, 2)), dma((RING, 2, 2)),
            dma((PLANE,)), dma((PLANE,)), dma((PLANE,)), dma((PLANE,)),
        ],
        compiler_params=pltpu.CompilerParams(
            collective_id=0, has_side_effects=True, vmem_limit_bytes=60 << 20
        ),
        name="exchange",
    )(irrep, i, j, k, occ, virt, virt, wm, wr, am)


def unpack_kernel(o_hbm, out_ref, o_ref, middle, sem, in_sem):
    low = lax.broadcasted_iota(jnp.int32, (8, LANES), 1) < PAD

    def place(src, tile, n):
        lanes = pl.ds(pl.multiple_of(tile * LANES, LANES), LANES)
        return pltpu.make_async_copy(src, out_ref.at[:, :, lanes], sem.at[n])

    def load(n):
        part = pl.ds(n * 2 * TILES, 2 * TILES)
        return pltpu.make_async_copy(o_hbm.at[part], o_ref.at[part], in_sem.at[n])

    for n in range(2):
        load(n).start()

    def pair(n, c):
        load(n).wait()
        pl.when(n + 2 < PLANE // 2)(lambda: load(n + 2).start())
        for t in range(TILES - 1):
            place(o_ref.at[n * 2 * TILES + t], n * 25 + t, 0).start()
            place(o_ref.at[n * 2 * TILES + TILES + 1 + t], n * 25 + TILES + t, 0).start()
        for m in range(HALVES):
            even = o_ref[n * 2 * TILES + TILES - 1, m].astype(F32)
            odd = o_ref[n * 2 * TILES + TILES, m].astype(F32)
            middle[n, 2 * m] = jnp.where(low, even, odd).astype(BF16)
            if m < HALVES - 1:
                middle[n, 2 * m + 1] = pltpu.roll(jnp.where(low, odd, even), PAD, 1).astype(BF16)
        place(middle.at[n], n * 25 + TILES - 1, 0).start()
        return c

    lax.fori_loop(0, PLANE // 2, pair, 0)
    pltpu.make_async_copy(out_ref, out_ref, sem.at[0]).wait()


def unpack(o):
    return pl.pallas_call(
        unpack_kernel,
        out_shape=jax.ShapeDtypeStruct((ROWS, HALF, RING * COLS * PLANE), BF16),
        in_specs=[pl.BlockSpec(memory_space=pl.ANY)],
        out_specs=pl.BlockSpec(memory_space=pl.ANY),
        scratch_shapes=[
            pltpu.VMEM((PLANE * TILES, ROWS, 8, LANES), BF16),
            pltpu.VMEM((PLANE // 2, ROWS, 8, LANES), BF16),
            pltpu.SemaphoreType.DMA((1,)),
            pltpu.SemaphoreType.DMA((PLANE // 2,)),
        ],
        compiler_params=pltpu.CompilerParams(vmem_limit_bytes=58 << 20),
        name="unpack",
    )(o)


def per_device(
    amplitudes, intermediate, occ_irrep, i_window, j_window, k_window, occ_energy, virt_energy
):
    wm, wr, am = pack(occ_irrep, k_window, intermediate.reshape(COLS, -1), amplitudes.transpose(1, 0, 2))
    o = exchange(
        occ_irrep, i_window, j_window, k_window, occ_energy, virt_energy, wm, wr, am
    )
    return unpack(o).transpose(1, 0, 2)


def solution(mesh):
    return jax.shard_map(
        per_device,
        mesh=mesh,
        in_specs=(P("rep", "tensor", None), P("tensor", None, "rep"), P(), P(), P(), P(), P(), P()),
        out_specs=P("rep", "tensor", None),
        check_vma=False,
    )
```
